32 devices in a mesh: dp: 16 (over z, y, core), fsdp: 2 (over x).
Axes of the slice: x: 2, y: 2, z: 4, core: 2. Of those that a mesh axis runs over, the one named last changes fastest.
Arguments:
- tokens: bfloat16 [8192, 1024], P(('dp', 'fsdp')), may hold values from -6 to 6
- image_ids: int32 [8192], P(('dp', 'fsdp')), may hold values from 0 to 5, as said below
- pad_mask: int32 [8192], P(('dp', 'fsdp')), may hold values from 0 to 1, as said below
- cotangent: bfloat16 [8192, 1024], P(('dp', 'fsdp')), may hold values from -6 to 6
- w_qkv: bfloat16 [2, 1024, 3072], P(None, 'fsdp'), may hold values from -0.1875 to 0.1875
- w_out: bfloat16 [2, 1024, 1024], P(None, 'fsdp'), may hold values from -6 to 6
- w_fc1: bfloat16 [2, 1024, 4096], P(None, 'fsdp'), may hold values from -0.1875 to 0.1875
- w_fc2: bfloat16 [2, 4096, 1024], P(None, 'fsdp'), may hold values from -0.09375 to 0.09375
- b_fc1: bfloat16 [2, 4096], P(None, 'fsdp'), may hold values from -3 to 3
- proj_bias: bfloat16 [2, 3, 1024], P(None, None, 'fsdp'), may hold values from -2 to 2
- value_bias: bfloat16 [2, 1024], P(None, 'fsdp'), may hold values from -0.3984375 to 0.3984375
- ln_gain: bfloat16 [2, 2, 1024], P(None, None, 'fsdp'), may hold values from 0.5 to 1.5
- ln_shift: bfloat16 [2, 2, 1024], P(None, None, 'fsdp'), may hold values from -1.1953125 to 1.1953125
- layer_scale: bfloat16 [2, 2, 1024], P(None, None, 'fsdp'), may hold values from 0.25 to 1
Outputs:
- output: bfloat16 [8192, 1024], P(('dp', 'fsdp'))
- input_grad: bfloat16 [8192, 1024], P(('dp', 'fsdp'))
- grad_w_qkv: float32 [2, 1024, 3072], P(None, 'fsdp')
- grad_w_out: float32 [2, 1024, 1024], P(None, 'fsdp')
- grad_w_fc1: float32 [2, 1024, 4096], P(None, 'fsdp')
- grad_w_fc2: float32 [2, 4096, 1024], P(None, 'fsdp')
- grad_b_fc1: float32 [2, 4096], P(None, 'fsdp')
- grad_proj_bias: float32 [2, 3, 1024], P(None, None, 'fsdp')
- grad_value_bias: float32 [2, 1024], P(None, 'fsdp')
- grad_ln_gain: float32 [2, 2, 1024], P(None, None, 'fsdp')
- grad_ln_shift: float32 [2, 2, 1024], P(None, None, 'fsdp')
- grad_layer_scale: float32 [2, 2, 1024], P(None, None, 'fsdp')
The draws below stay inside these ranges and needn't reach their ends.
Inputs may be any that keep to these rules, and one draw needn't show every extreme that they name: `image_ids`: images are runs of exactly 1370 consecutive tokens numbered 0 to 4 in stream order; runs of padding tokens lie between some of them and after them and carry the number 5. pad_mask is 1 exactly on the tokens whose image number is below 5.
All inputs are finite; a program needn't handle non-finite values.
Results may differ from the reference program's by a relative error of at most 0.017.
Values may be sent and summed in bfloat16 or wider, within the bound.
No kernel may reach another device: no remote copies, remote signals or barrier semaphores. Data moves between devices by JAX's collectives and lax.ppermute only.
A program may use at most 320 MiB of HBM per device.

```python
import math
import jax
import jax.numpy as jnp
from jax import lax

D = 1024
HEADS = 16
HD = 64
FF = 4096
IMG = 1370
LAYERS = 2
TOK_DEV = 256
REACH = 6
TOKENS = 8192


def bin_counts(draws, bin_total):
    bins = jnp.arange(bin_total, dtype=jnp.int32)
    return jnp.sum((draws[:, None] == bins[None, :]).astype(jnp.int32), axis=0)


def packing(key):
    inner = jax.random.fold_in(key, 11)
    images_total = TOKENS // IMG
    spare_tokens = TOKENS - images_total * IMG
    middle_dev = TOKENS // TOK_DEV // 2
    first_start = max(0, middle_dev * TOK_DEV - IMG + 1)
    residue = first_start % IMG
    if residue <= spare_tokens:
        anchor_start = first_start
    else:
        anchor_start = first_start + IMG - residue
    lead_images = min(anchor_start // IMG, images_total - 2)
    before_pad = min(anchor_start - lead_images * IMG, spare_tokens)
    needed_gap = max(0, (middle_dev + REACH) * TOK_DEV - anchor_start - 2 * IMG + 1)
    between_pad = min(needed_gap, spare_tokens - before_pad)
    after_pad = spare_tokens - before_pad - between_pad
    before_draw = jax.random.randint(jax.random.fold_in(inner, 1), (before_pad,), 0, lead_images + 1)
    after_draw = jax.random.randint(jax.random.fold_in(inner, 2), (after_pad,), lead_images + 2, images_total + 1)
    gap_index = jnp.arange(images_total + 1, dtype=jnp.int32)
    gap_sizes = bin_counts(before_draw, images_total + 1) + bin_counts(after_draw, images_total + 1) + between_pad * (gap_index == lead_images + 1).astype(jnp.int32)
    image_starts = jnp.arange(images_total, dtype=jnp.int32) * IMG + jnp.cumsum(gap_sizes)[:images_total].astype(jnp.int32)
    positions = jnp.arange(TOKENS, dtype=jnp.int32)
    image_index = jnp.sum((image_starts[None, :] <= positions[:, None]).astype(jnp.int32), axis=1) - 1
    first_token = image_starts[jnp.maximum(image_index, 0)]
    inside = (image_index >= 0) & (positions < first_token + IMG)
    return (jnp.where(inside, image_index, images_total).astype(jnp.int32), inside.astype(jnp.int32))


def draw_image_ids(key, part):
    return packing(key)[0]


def draw_pad_mask(key, part):
    return packing(key)[1]


def block_levels(own_key, dims, cuts, smallest, high):
    level, own = 1.0, jax.random.fold_in(own_key, 6)
    for dim, parts in cuts:
        steps = jnp.exp(jax.random.uniform(jax.random.fold_in(own, dim), (parts,), jnp.float32, smallest / len(cuts), high / len(cuts)))
        level = level * jnp.repeat(steps, dims[dim] // parts).reshape([-1 if axis == dim else 1 for axis in range(len(dims))])
    return level


def gaussian(stream_key, dims, deviation, limit, cuts=(), kind=jnp.bfloat16):
    values = jax.random.normal(stream_key, dims, jnp.float32) * deviation
    if len(cuts) > 0:
        values = block_levels(stream_key, dims, cuts, -0.22, 0.18) * values
    return jnp.clip(values, min=-limit, max=limit).astype(kind)


def setup_inputs(seed: int = 0) -> dict:
    arg_keys = jax.random.split(jax.random.key(seed), 15)
    return {
        "tokens": gaussian(arg_keys[0], (TOKENS, D), 1.0, 6.0, ((0, 32),)),
        "image_ids": draw_image_ids(jax.random.fold_in(arg_keys[14], 71), 0),
        "pad_mask": draw_pad_mask(jax.random.fold_in(arg_keys[14], 71), 0),
        "cotangent": gaussian(arg_keys[3], (TOKENS, D), 1.0, 6.0, ((0, 32),)),
        "w_qkv": gaussian(arg_keys[4], (LAYERS, D, 3 * D), D ** -0.5, 0.1875, ((1, 2),)),
        "w_out": gaussian(arg_keys[5], (LAYERS, D, D), (max(1, 2 * D // IMG)) ** -0.5, 6.0, ((1, 2),)),
        "w_fc1": gaussian(arg_keys[6], (LAYERS, D, FF), D ** -0.5, 0.1875, ((1, 2),)),
        "w_fc2": gaussian(arg_keys[7], (LAYERS, FF, D), FF ** -0.5, 0.09375, ((1, 2),)),
        "b_fc1": gaussian(arg_keys[8], (LAYERS, FF), 0.5, 3.0, ((1, 2),)),
        "proj_bias": gaussian(arg_keys[9], (LAYERS, 3, D), 0.3, 2.0, ((2, 2),)),
        "value_bias": gaussian(arg_keys[10], (LAYERS, D), 0.06, 0.3984375, ((1, 2),)),
        "ln_gain": jnp.clip(1.0 + 0.1 * jax.random.normal(arg_keys[11], (LAYERS, 2, D), jnp.float32), 0.5, 1.5).astype(jnp.bfloat16),
        "ln_shift": gaussian(arg_keys[12], (LAYERS, 2, D), 0.2, 1.1953125, ((2, 2),)),
        "layer_scale": jnp.clip(jnp.exp(math.log(1.0) - 1.3862944 * jax.random.uniform(arg_keys[13], (LAYERS, 2, D), jnp.float32) ** block_levels(arg_keys[13], (LAYERS, 2, D), ((2, 2),), -0.2, 0.2)), 0.25, 1.0).astype(jnp.bfloat16),
    }


highest = lax.Precision.HIGHEST

@jax.custom_vjp
def low(v):
    return lax.optimization_barrier(v.astype(jnp.bfloat16)).astype(jnp.float32)

@jax.custom_vjp
def low_back(v):
    return v

def low_keep(v):
    return (low(v), None)

def low_pass(kept, grad):
    return (grad,)

def back_keep(v):
    return (v, None)

def back_low(kept, grad):
    return (low(grad),)
low.defvjp(low_keep, low_pass)
low_back.defvjp(back_keep, back_low)

def both_ways(values):
    return low_back(low(values))

def layer_norm(values, gain_row, shift_row):
    centre = values - lax.optimization_barrier(jnp.mean(values, axis=-1, keepdims=True))
    spread = lax.optimization_barrier(jnp.mean(centre * centre, axis=-1, keepdims=True))
    return centre * lax.rsqrt(spread + 1e-06) * gain_row + shift_row

def attention(queries, key_rows, value_rows, image_ids, pad_mask):
    margin = REACH * TOK_DEV
    key_span = (2 * REACH + 1) * TOK_DEV
    key_pad = jnp.pad(key_rows, ((margin, margin), (0, 0)))
    value_pad = jnp.pad(value_rows, ((margin, margin), (0, 0)))
    id_pad = jnp.pad(image_ids, (margin, margin), constant_values=-1)
    live_pad = jnp.pad(pad_mask, (margin, margin))
    columns = jnp.arange(key_span, dtype=jnp.int32)
    row_place = jnp.arange(TOK_DEV, dtype=jnp.int32)
    own_place = columns[None, :] == row_place[:, None] + margin

    def block(block_index):
        block_start = (block_index * TOK_DEV).astype(jnp.int32)
        query_blk = lax.dynamic_slice_in_dim(queries, block_start, TOK_DEV, 0).reshape(TOK_DEV, HEADS, HD)
        key_blk = lax.dynamic_slice_in_dim(key_pad, block_start, key_span, 0).reshape(key_span, HEADS, HD)
        value_blk = lax.dynamic_slice_in_dim(value_pad, block_start, key_span, 0).reshape(key_span, HEADS, HD)
        query_ids = lax.dynamic_slice_in_dim(image_ids, block_start, TOK_DEV, 0)
        key_ids = lax.dynamic_slice_in_dim(id_pad, block_start, key_span, 0)
        key_live = lax.dynamic_slice_in_dim(live_pad, block_start, key_span, 0)
        allowed = (query_ids[:, None] == key_ids[None, :]) & (key_live[None, :] == 1) | own_place
        scores = low_back(jnp.einsum('qhd,khd->hqk', query_blk, key_blk, precision=highest) * 0.125)
        scores = jnp.where(allowed[None], scores, -1e+30)
        row_top = lax.optimization_barrier(jnp.max(scores, axis=-1, keepdims=True))
        exponent = jnp.exp(scores - row_top)
        soft_probs = low(exponent / lax.optimization_barrier(jnp.sum(exponent, axis=-1, keepdims=True)))
        mixed_heads = jnp.einsum('hqk,khd->qhd', soft_probs, value_blk, precision=highest)
        return mixed_heads.reshape(TOK_DEV, HEADS * HD)
    blocks = lax.map(jax.checkpoint(block), jnp.arange(TOKENS // TOK_DEV, dtype=jnp.int32))
    return blocks.reshape(TOKENS, HEADS * HD)

def forward(residual, w_qkv, w_out, w_fc1, w_fc2, b_fc1, proj_bias, value_bias, ln_gain, ln_shift, layer_scale, image_ids, pad_mask):
    for layer_idx in range(LAYERS):
        normed = low(layer_norm(residual, ln_gain[layer_idx, 0], ln_shift[layer_idx, 0]))
        projected = jnp.dot(normed, w_qkv[layer_idx], precision=highest, preferred_element_type=jnp.float32)
        queries = both_ways(projected[:, :D] + proj_bias[layer_idx, 0])
        key_rows = both_ways(projected[:, D:2 * D])
        value_rows = both_ways(projected[:, 2 * D:] + value_bias[layer_idx])
        mixed = both_ways(attention(queries, key_rows, value_rows, image_ids, pad_mask))
        branch = low_back(jnp.dot(mixed, w_out[layer_idx], precision=highest, preferred_element_type=jnp.float32) + proj_bias[layer_idx, 1])
        residual = residual + layer_scale[layer_idx, 0] * branch
        normed = low(layer_norm(residual, ln_gain[layer_idx, 1], ln_shift[layer_idx, 1]))
        hidden = low_back(jnp.dot(normed, w_fc1[layer_idx], precision=highest, preferred_element_type=jnp.float32) + b_fc1[layer_idx])
        active = low(jax.nn.gelu(hidden, approximate=False))
        branch = low_back(jnp.dot(active, w_fc2[layer_idx], precision=highest, preferred_element_type=jnp.float32) + proj_bias[layer_idx, 2])
        residual = residual + layer_scale[layer_idx, 1] * branch
    return residual

def reference(tokens, image_ids, pad_mask, cotangent, w_qkv, w_out, w_fc1, w_fc2, b_fc1, proj_bias, value_bias, ln_gain, ln_shift, layer_scale):
    floats = [piece.astype(jnp.float32) for piece in (tokens, w_qkv, w_out, w_fc1, w_fc2, b_fc1, proj_bias, value_bias, ln_gain, ln_shift, layer_scale)]

    def wrapped(*pieces):
        return forward(*pieces, image_ids, pad_mask)
    result, pullback = jax.vjp(wrapped, *floats)
    gradients = pullback(cotangent.astype(jnp.float32))
    return (result.astype(jnp.bfloat16), gradients[0].astype(jnp.bfloat16), gradients[1], gradients[2], gradients[3], gradients[4], gradients[5], gradients[6], gradients[7], gradients[8], gradients[9], gradients[10])
```

```python
import jax
import jax.numpy as jnp
from jax import lax
from jax.experimental import pallas as pl
from jax.experimental.pallas import tpu as pltpu
from jax.sharding import Mesh
from jax.sharding import PartitionSpec as P


HD = 64
LAYERS = 2
REACH = 6
GROUP = 8
LANES = 128
KEYS = 1536
KEYS_BACK = 768
BF = jnp.bfloat16
F32 = jnp.float32
ALL = ("z", "y", "c", "x")

QKV, OUT, FC1, FC2 = range(4)
UNITS = ((QKV, 0, 3), (QKV, 0, 1), (QKV, 1, 2), (OUT, 0, 1), (FC1, 0, 2), (FC1, 2, 2), (FC2, 0, 2), (FC2, 2, 2))
NQKV, NQ, NKV, NOUT, FC1A, FC1B, FC2A, FC2B = range(8)
GROUPS = ((NOUT, NQKV), (FC1A, FC1B), (FC2A, FC2B), (NOUT, NQ), (NKV,))
GQ, G1, G2, GA, GB = range(5)
USED = ((G2, G1, GA, GB), (G2, G1, GQ))
BY_HAND = ((G2, 0), (GA, 0), (GB, 0))


DP = ("z", "y", "c")


def layer_norm(values, gain_row, shift_row):
    centre = values - jnp.mean(values, axis=-1, keepdims=True)
    spread = jnp.mean(centre * centre, axis=-1, keepdims=True)
    return centre * lax.rsqrt(spread + 1e-06) * gain_row + shift_row


def nn(a, b):
    return lax.dot_general(a, b, (((1,), (0,)), ((), ())), preferred_element_type=F32)


def nt(a, b):
    return lax.dot_general(a, b, (((1,), (1,)), ((), ())), preferred_element_type=F32)


def tn(a, b):
    return lax.dot_general(a, b, (((0,), (0,)), ((), ())), preferred_element_type=F32)


def masked_heads(value, low):
    return jnp.concatenate([jnp.where(low, value, 0.0), jnp.where(low, 0.0, value)], axis=0).astype(BF)


def key_range(lo_ref, hi_ref, blocks, chunk):
    i = pl.program_id(0)
    trips = (hi_ref[i] - lo_ref[i] + chunk - 1) // chunk
    return jnp.minimum(lo_ref[i], blocks - trips * chunk), trips


def attn_fwd_kernel(lo_ref, hi_ref, q_ref, k_ref, v_ref, qid_ref, kid_ref, o_ref, of_ref, lse_ref, s_scr, m_scr, l_scr, a_scr):
    blk = q_ref.shape[0]
    span = s_scr.shape[2]
    chunk = span // LANES
    low = lax.broadcasted_iota(jnp.int32, (blk, 2 * HD), 1) < HD
    q2 = masked_heads(q_ref[...].astype(F32) * 0.125, low)
    qid = qid_ref[...]
    qid2 = jnp.broadcast_to(jnp.concatenate([qid, qid], axis=0), (2 * blk, LANES))
    lo, trips = key_range(lo_ref, hi_ref, kid_ref.shape[0], chunk)
    m_scr[...] = jnp.full_like(m_scr, -1e30)
    l_scr[...] = jnp.zeros_like(l_scr)
    a_scr[...] = jnp.zeros_like(a_scr)

    def scores(t, carry):
        at = lo + t * chunk
        s = nt(q2, k_ref[pl.ds(pl.multiple_of(at * LANES, LANES), span), :])
        top = m_scr[...]
        for part in range(chunk):
            cols = slice(part * LANES, (part + 1) * LANES)
            piece = jnp.where(qid2 == kid_ref[at + part], s[:, cols], -1e30)
            s_scr[t, :, cols] = piece
            top = jnp.maximum(top, piece)
        m_scr[...] = top
        return carry

    lax.fori_loop(0, trips, scores, 0)
    row_top = jnp.max(m_scr[...], axis=1, keepdims=True)
    top = jnp.broadcast_to(row_top, (2 * blk, LANES))

    def mix(t, carry):
        v = v_ref[pl.ds(pl.multiple_of((lo + t * chunk) * LANES, LANES), span), :]
        total = l_scr[...]
        probs = []
        for part in range(chunk):
            p = jnp.exp(s_scr[t, :, part * LANES : (part + 1) * LANES] - top)
            total = total + p
            probs.append(p.astype(BF))
        l_scr[...] = total
        a_scr[...] += nn(jnp.concatenate(probs, axis=1), v)
        return carry

    lax.fori_loop(0, trips, mix, 0)
    row_total = jnp.sum(l_scr[...], axis=1, keepdims=True)
    out = a_scr[...] / row_total
    mixed = jnp.where(low, out[:blk], out[blk:])
    o_ref[...] = mixed.astype(BF)
    of_ref[...] = mixed
    lse = jnp.broadcast_to(row_top + jnp.log(row_total), (2 * blk, LANES))
    lse_ref[0] = jnp.transpose(lse)[0:1, :]


def attn_fwd(qkv, kv_win, qid_col, kid_row, lo, hi):
    rows = qkv.shape[0]
    blk = rows // lo.shape[0]
    span = kv_win.shape[0]
    wide = 2 * HD
    most = -(-((2 * REACH + 1) * blk + LANES) // KEYS)
    pairs = rows * blk * 7 * 2
    return pl.pallas_call(
        attn_fwd_kernel,
        grid_spec=pltpu.PrefetchScalarGridSpec(
            num_scalar_prefetch=2,
            grid=(rows // blk,),
            in_specs=[
                pl.BlockSpec((blk, wide), lambda i, lo, hi: (i, 0)),
                pl.BlockSpec((span, wide), lambda i, lo, hi: (0, 0)),
                pl.BlockSpec((span, wide), lambda i, lo, hi: (0, 1)),
                pl.BlockSpec((blk, 1), lambda i, lo, hi: (i, 0)),
                pl.BlockSpec(kid_row.shape, lambda i, lo, hi: (0, 0, 0)),
            ],
            out_specs=[
                pl.BlockSpec((blk, wide), lambda i, lo, hi: (i, 0)),
                pl.BlockSpec((blk, wide), lambda i, lo, hi: (i, 0)),
                pl.BlockSpec((1, 1, 2 * blk), lambda i, lo, hi: (i, 0, 0)),
            ],
            scratch_shapes=[pltpu.VMEM((most, 2 * blk, KEYS), F32)] + [pltpu.VMEM((2 * blk, LANES), F32)] * 3,
        ),
        out_shape=[
            jax.ShapeDtypeStruct((rows, wide), BF),
            jax.ShapeDtypeStruct((rows, wide), F32),
            jax.ShapeDtypeStruct((rows // blk, 1, 2 * blk), F32),
        ],
        cost_estimate=pl.CostEstimate(
            flops=pairs * wide * 4, bytes_accessed=span * wide * 4 + rows * wide * 8, transcendentals=pairs
        ),
        name="attn_fwd",
    )(lo, hi, qkv, kv_win, kv_win, qid_col, kid_row)


def attn_bwd_kernel(
    lo_ref, hi_ref, q_ref, k_ref, v_ref, do_ref, qid_ref, kid_ref, lse_ref, of_ref, dq_ref, own_ref, prev_ref, next_ref, dk_scr, dv_scr, dq_scr
):
    blk = q_ref.shape[0]
    i = pl.program_id(0)
    halo = prev_ref.shape[0]
    rows = own_ref.shape[0]
    wide = 2 * HD
    low = lax.broadcasted_iota(jnp.int32, (blk, wide), 1) < HD

    @pl.when(i == 0)
    def _():
        dk_scr[...] = jnp.zeros_like(dk_scr)
        dv_scr[...] = jnp.zeros_like(dv_scr)

    q2 = masked_heads(q_ref[...].astype(F32) * 0.125, low)
    grad = do_ref[...].astype(F32)
    g2 = masked_heads(grad, low)
    picks = jnp.where(lax.broadcasted_iota(jnp.int32, (8, wide), 1) < HD, 1.0, 0.0)
    dots = [
        lax.dot_general(
            pick, grad * of_ref[...], (((1,), (1,)), ((), ())), precision=lax.Precision.HIGHEST, preferred_element_type=F32
        )
        for pick in (picks, 1.0 - picks)
    ]
    dd = jnp.concatenate([d[0:1] for d in dots], axis=1)
    qid = qid_ref[0]
    lse = lse_ref[0]
    chunk = KEYS_BACK // LANES
    lo, trips = key_range(lo_ref, hi_ref, k_ref.shape[0] // LANES, chunk)
    dq_scr[...] = jnp.zeros_like(dq_scr)

    def step(t, carry):
        at = pl.ds(pl.multiple_of((lo + t * chunk) * LANES, LANES), KEYS_BACK)
        k = k_ref[at, :]
        v = v_ref[at, :]
        s = nt(k, q2)
        p = jnp.where(kid_ref[at, :] == qid, jnp.exp(s - lse), 0.0)
        dp = nt(v, g2)
        ds = (p * (dp - dd)).astype(BF)
        dv_scr[at, :] += nn(p.astype(BF), g2)
        dk_scr[at, :] += nn(ds, q2)
        dq_scr[...] += tn(ds, k)
        return carry

    lax.fori_loop(0, trips, step, 0)
    dq = dq_scr[...]
    dq_ref[...] = (jnp.where(low, dq[:blk], dq[blk:]) * 0.125).astype(BF)

    @pl.when(i == pl.num_programs(0) - 1)
    def _():
        for side, scr in enumerate((dk_scr, dv_scr)):
            cols = pl.ds(side * wide, wide)
            prev_ref[:, cols] = scr[pl.ds(0, halo), :].astype(BF)
            own_ref[:, cols] = scr[pl.ds(halo, rows), :]
            next_ref[:, cols] = scr[pl.ds(halo + rows, halo), :].astype(BF)


def attn_bwd(qkv, kv_win, grad_out, qid_row, kid_col, lse, mixed, lo, hi):
    rows = qkv.shape[0]
    blk = rows // qid_row.shape[0]
    span = kv_win.shape[0]
    halo = (span - rows) // 2
    wide = 2 * HD
    pairs = rows * blk * 7 * 2
    row_spec = pl.BlockSpec((1, 1, 2 * blk), lambda i, lo, hi: (i, 0, 0))
    return pl.pallas_call(
        attn_bwd_kernel,
        grid_spec=pltpu.PrefetchScalarGridSpec(
            num_scalar_prefetch=2,
            grid=(rows // blk,),
            in_specs=[
                pl.BlockSpec((blk, wide), lambda i, lo, hi: (i, 0)),
                pl.BlockSpec((span, wide), lambda i, lo, hi: (0, 0)),
                pl.BlockSpec((span, wide), lambda i, lo, hi: (0, 1)),
                pl.BlockSpec((blk, wide), lambda i, lo, hi: (i, 0)),
                row_spec,
                pl.BlockSpec((span, 1), lambda i, lo, hi: (0, 0)),
                row_spec,
                pl.BlockSpec((blk, wide), lambda i, lo, hi: (i, 0)),
            ],
            out_specs=[
                pl.BlockSpec((blk, wide), lambda i, lo, hi: (i, 0)),
                pl.BlockSpec((rows, 2 * wide), lambda i, lo, hi: (0, 0)),
                pl.BlockSpec((halo, 2 * wide), lambda i, lo, hi: (0, 0)),
                pl.BlockSpec((halo, 2 * wide), lambda i, lo, hi: (0, 0)),
            ],
            scratch_shapes=[pltpu.VMEM((span, wide), F32)] * 2 + [pltpu.VMEM((2 * blk, wide), F32)],
        ),
        out_shape=[
            jax.ShapeDtypeStruct((rows, wide), BF),
            jax.ShapeDtypeStruct((rows, 2 * wide), F32),
            jax.ShapeDtypeStruct((halo, 2 * wide), BF),
            jax.ShapeDtypeStruct((halo, 2 * wide), BF),
        ],
        cost_estimate=pl.CostEstimate(
            flops=pairs * wide * 10, bytes_accessed=span * wide * 12 + rows * wide * 12, transcendentals=pairs
        ),
        name="attn_bwd",
    )(lo, hi, qkv, kv_win, kv_win, grad_out, qid_row, kid_col, lse, mixed)


def lanes(start, size):
    return pl.ds(pl.multiple_of(start, 128), size)


def gelu_parts(values):
    share = 0.5 * (1.0 + lax.erf(values * 0.7071067811865476))
    slope = share + values * (0.3989422804014327 * jnp.exp(-0.5 * values * values))
    return values * share, slope


def halves_sum(start_ref, acts_ref, own_ref, other_refs):
    total = nn(acts_ref[:, lanes(start_ref[0], own_ref.shape[1])], own_ref[0])
    for k, ref in enumerate(other_refs):
        total += nn(acts_ref[:, lanes(start_ref[k + 1], ref.shape[0])], ref[...])
    return total


def qkv_kernel(start_ref, acts_ref, own_ref, *refs):
    others, bias_ref, out_ref = refs[:-2], refs[-2], refs[-1]
    proj = halves_sum(start_ref, acts_ref, own_ref, others) + bias_ref[0]
    wide = out_ref.shape[2]
    for g in range(GROUP):
        out_ref[g] = proj[:, g * wide : (g + 1) * wide].astype(BF)


def fc1_kernel(start_ref, acts_ref, own_ref, *refs):
    others, bias_ref, active_ref, slope_ref = refs[:-3], *refs[-3:]
    value, slope = gelu_parts(halves_sum(start_ref, acts_ref, own_ref, others) + bias_ref[0])
    active_ref[...] = value.astype(BF)
    slope_ref[...] = slope.astype(BF)


def plain_kernel(start_ref, acts_ref, own_ref, *refs):
    others, bias_ref, out_ref = refs[:-2], refs[-2], refs[-1]
    out_ref[...] = halves_sum(start_ref, acts_ref, own_ref, others) + bias_ref[0]


def other_spec(tall, wide, at):
    first = at // wide
    return pl.BlockSpec((tall, wide), lambda j, start: (0, first + j))


def product(kernel, acts, own, layer, others, starts, wide, bias, out_specs, out_shape):
    tokens = acts.shape[0]
    tall, width = own.shape[1:]
    steps = width // wide
    return pl.pallas_call(
        kernel,
        grid_spec=pltpu.PrefetchScalarGridSpec(
            num_scalar_prefetch=1,
            grid=(steps,),
            in_specs=[
                pl.BlockSpec(acts.shape, lambda j, start: (0, 0)),
                pl.BlockSpec((1, tall, wide), lambda j, start: (layer, 0, j)),
                *[other_spec(rows, wide, at) for _, rows, at in others],
                pl.BlockSpec((1, 1, wide), lambda j, start: (j, 0, 0)),
            ],
            out_specs=out_specs,
        ),
        out_shape=out_shape,
        cost_estimate=pl.CostEstimate(
            flops=4 * tokens * tall * width, bytes_accessed=4 * tall * width + 6 * tokens * width, transcendentals=0
        ),
    )(starts, acts, own, *[array for array, _, _ in others], bias.reshape(steps, 1, wide))


def gact_kernel(start_ref, grad_ref, own_ref, *refs):
    others, slope_ref, out_ref, sum_ref = refs[:-3], *refs[-3:]
    weights = [own_ref[0]] + [ref[...] for ref in others]
    for n, weight in enumerate(weights):
        at = lanes(start_ref[n] + pl.program_id(0) * weight.shape[0], weight.shape[0])
        grad = (nt(grad_ref[...], weight) * slope_ref[:, at].astype(F32)).astype(BF)
        out_ref[:, at] = grad
        sum_ref[:, at] = jnp.sum(grad.astype(F32), axis=0, keepdims=True)


def dx_kernel(start_ref, grad_ref, own_ref, other_refs, out_ref):
    weights = [own_ref[0]] + [ref[...] for ref in other_refs]
    for n, weight in enumerate(weights):
        at = lanes(start_ref[n], weight.shape[0])
        term = nt(grad_ref[...], weight)

        @pl.when(pl.program_id(0) == 0)
        def _():
            out_ref[:, at] = term

        @pl.when(pl.program_id(0) > 0)
        def _():
            out_ref[:, at] += term


def dx_plain_kernel(start_ref, grad_ref, own_ref, *refs):
    dx_kernel(start_ref, grad_ref, own_ref, refs[:-1], refs[-1])


def dx_qkv_kernel(start_ref, heads_ref, own_ref, *refs):
    others, out_ref, grad_ref = refs[:-2], refs[-2], refs[-1]
    wide = heads_ref.shape[2]
    for g in range(GROUP):
        grad_ref[:, g * wide : (g + 1) * wide] = heads_ref[g]
    dx_kernel(start_ref, grad_ref, own_ref, others, out_ref)


def dx_out_kernel(start_ref, grad_ref, own_ref, *refs):
    others, out_ref, scr = refs[:-2], refs[-2], refs[-1]
    dx_kernel(start_ref, grad_ref, own_ref, others, scr)
    wide = out_ref.shape[2]

    @pl.when(pl.program_id(0) == pl.num_programs(0) - 1)
    def _():
        for g in range(GROUP):
            out_ref[g] = scr[:, g * wide : (g + 1) * wide].astype(BF)


def product_back(kernel, grad, grad_spec, own, layer, others, starts, wide, out_specs, out_shape, scratch=()):
    tall, width = own.shape[1:]
    return pl.pallas_call(
        kernel,
        grid_spec=pltpu.PrefetchScalarGridSpec(
            num_scalar_prefetch=1,
            grid=(width // wide,),
            in_specs=[
                grad_spec,
                pl.BlockSpec((1, tall, wide), lambda j, start: (layer, 0, j)),
                *[other_spec(rows, wide, at) for _, rows, at in others],
            ],
            out_specs=out_specs,
            scratch_shapes=list(scratch),
        ),
        out_shape=out_shape,
        cost_estimate=pl.CostEstimate(
            flops=1024 * tall * width, bytes_accessed=4 * tall * width + 1024 * (tall + width), transcendentals=0
        ),
    )(starts, grad, own, *[array for array, _, _ in others])


QUARTER = 256
WIDE = 1024


def split_rows(scr, side, keep_ref, away_ref):
    half = keep_ref.shape[0]
    keep_ref[...] = scr[pl.ds(pl.multiple_of(side * half, half), half), :].astype(BF)
    away_ref[...] = scr[pl.ds(pl.multiple_of((1 - side) * half, half), half), :].astype(BF)


def away_kernel(spot_ref, mine_ref, theirs_ref, cols_ref, cols2_ref, out_ref):
    out_ref[...] = (tn(mine_ref[...], cols_ref[...]) + tn(theirs_ref[...], cols2_ref[...])).astype(BF)


def keep_kernel(spot_ref, mine_ref, theirs_ref, cols_ref, cols2_ref, came_ref, *refs):
    keep_ref, away_ref, scr = refs[-3:]
    scr[...] = tn(mine_ref[...], cols_ref[...]) + tn(theirs_ref[...], cols2_ref[...]) + came_ref[...].astype(F32)
    split_rows(scr, spot_ref[2], keep_ref, away_ref)


def block_grad(mine, theirs, cols, cols2, spot, first, steps, came=None, into=None, at=0, whole=0):
    tokens, depth = mine.shape
    width = cols.shape[1]
    subs = depth // (4 * QUARTER)
    over = (lambda j: 0) if subs > 1 else (lambda j: first + j)
    sub = (lambda j: first + j) if subs > 1 else (lambda j: 0)
    col = pl.BlockSpec((tokens, WIDE), lambda j, spot: (0, over(j)))
    in_specs = [
        pl.BlockSpec((tokens, QUARTER), lambda j, spot: (0, (spot[0] * 2 + spot[1]) * subs + sub(j))),
        pl.BlockSpec((tokens, QUARTER), lambda j, spot: (0, spot[0] * subs + sub(j))),
        col,
        col,
    ]
    operands = [mine, theirs, cols, cols2]
    scratch = []
    aliases = {}
    if came is None:
        kernel = away_kernel
        out_specs = pl.BlockSpec((QUARTER, WIDE), lambda j, spot: (0, j))
        out_shape = jax.ShapeDtypeStruct((QUARTER, steps * WIDE), BF)
    else:
        kernel = keep_kernel
        in_specs.append(pl.BlockSpec((QUARTER, WIDE), lambda j, spot: (0, j)))
        operands.append(came)
        out_specs = [pl.BlockSpec((QUARTER // 2, WIDE), lambda j, spot: (0, at // WIDE + j))] * 2
        out_shape = [jax.ShapeDtypeStruct((QUARTER // 2, whole), BF)] * 2
        scratch = [pltpu.VMEM((QUARTER, WIDE), F32)]
        if into is not None:
            in_specs += [pl.BlockSpec(memory_space=pl.ANY)] * 2
            operands += into
            aliases = {6: 0, 7: 1}
    return pl.pallas_call(
        kernel,
        grid_spec=pltpu.PrefetchScalarGridSpec(
            num_scalar_prefetch=1, grid=(steps,), in_specs=in_specs, out_specs=out_specs, scratch_shapes=scratch
        ),
        out_shape=out_shape,
        input_output_aliases=aliases,
        cost_estimate=pl.CostEstimate(
            flops=4 * tokens * QUARTER * steps * WIDE, bytes_accessed=2 * tokens * (depth + 2 * width), transcendentals=0
        ),
    )(spot, *operands)


def sum_y_kernel(at_ref, held_ref, came_ref, *refs):
    outs, scr = refs[:-1], refs[-1]
    scr[...] = held_ref[...].astype(F32) + came_ref[...].astype(F32)
    tall = outs[0].shape[0]
    for n, out_ref in enumerate(outs):
        out_ref[...] = scr[pl.ds(pl.multiple_of(at_ref[n] * tall, tall), tall), :].astype(BF)


def sum_z_kernel(*refs):
    total = refs[0][...].astype(F32)
    for ref in refs[1:-1]:
        total += ref[...].astype(F32)
    refs[-1][...] = total.astype(BF)


def sum_y(held, came, order):
    tall, width = held.shape
    count = order.shape[0]
    wide = 2048
    spec = pl.BlockSpec((tall, wide), lambda j, at: (0, j))
    return pl.pallas_call(
        sum_y_kernel,
        grid_spec=pltpu.PrefetchScalarGridSpec(
            num_scalar_prefetch=1,
            grid=(width // wide,),
            in_specs=[spec, spec],
            out_specs=[pl.BlockSpec((tall // count, wide), lambda j, at: (0, j))] * count,
            scratch_shapes=[pltpu.VMEM((tall, wide), F32)],
        ),
        out_shape=[jax.ShapeDtypeStruct((tall // count, width), BF)] * count,
        cost_estimate=pl.CostEstimate(flops=tall * width, bytes_accessed=6 * tall * width, transcendentals=0),
    )(order, held, came)


def sum_z(parts):
    tall, width = parts[0].shape
    wide = 2048
    spec = pl.BlockSpec((tall, wide), lambda j: (0, j))
    return pl.pallas_call(
        sum_z_kernel,
        grid=(width // wide,),
        in_specs=[spec] * len(parts),
        out_specs=spec,
        out_shape=jax.ShapeDtypeStruct((tall, width), BF),
        cost_estimate=pl.CostEstimate(flops=4 * tall * width, bytes_accessed=10 * tall * width, transcendentals=0),
    )(*parts)


def place_kernel(spans, z_major, spot_ref, in_ref, *refs):
    outs = refs[-len(spans) :]
    count = in_ref.shape[0 if z_major else 1]
    share = in_ref.shape[2]
    for z in range(count):
        rows = pl.ds(pl.multiple_of(spot_ref[z] * share, share), share)
        for (at, subs, _, _), out_ref in zip(spans, outs, strict=True):
            wide = out_ref.shape[5]
            for k in range(subs):
                cols = slice(at + k * wide, at + (k + 1) * wide)
                piece = in_ref[z, 0, :, cols] if z_major else in_ref[0, z, :, cols]
                out_ref[0, 0, k, 0, rows, :] = piece.astype(F32)


def place_rows(gathered, z_major, spots, spans, layer, wholes):
    count, sides = gathered.shape[:2] if z_major else gathered.shape[1::-1]
    share, width = gathered.shape[2:]
    rows = count * share
    steps = width // WIDE if len(spans) == 1 and spans[0][3] is not None else 1
    part = width // steps
    block = (count, 1, share, part) if z_major else (1, count, share, part)
    shapes = [jax.ShapeDtypeStruct((LAYERS, 2, subs, 2, rows, wide), F32) for _, subs, wide, _ in spans]
    more = [] if wholes[0] is None else wholes

    def out_spec(span):
        _, subs, wide, first = span
        wide, at = (wide, 0) if first is None else (WIDE, first)
        return pl.BlockSpec(
            (1, 1, subs, 1, rows, wide), lambda b, j, spot: (layer, spot[count + b], 0, spot[count + sides + b], 0, at + j)
        )

    return pl.pallas_call(
        lambda *refs: place_kernel(spans, z_major, *refs),
        grid_spec=pltpu.PrefetchScalarGridSpec(
            num_scalar_prefetch=1,
            grid=(sides, steps),
            in_specs=[pl.BlockSpec(block, lambda b, j, spot: (0, b, 0, j) if z_major else (b, 0, 0, j))]
            + [pl.BlockSpec(memory_space=pl.ANY)] * len(more),
            out_specs=[out_spec(span) for span in spans],
        ),
        out_shape=shapes,
        input_output_aliases={n + 2: n for n in range(len(more))},
        cost_estimate=pl.CostEstimate(flops=0, bytes_accessed=6 * count * sides * share * width, transcendentals=0),
    )(spots, gathered, *more)


def build(sizes):
    group_axes = []
    reach = 1
    for name in reversed(ALL):
        if reach < GROUP:
            group_axes.insert(0, name)
            reach *= sizes[name]
    assert reach == GROUP
    group_axes = tuple(group_axes)
    total = sizes["z"] * sizes["y"] * sizes["c"] * sizes["x"]
    pairwise = sizes["x"] == 2 and sizes["z"] == 4

    def flip(value, axis, bit):
        return lax.ppermute(value, axis, [(i, i ^ bit) for i in range(sizes[axis])])

    def shift_groups(value, by):
        pairs = [(i, i + by * GROUP) for i in range(total) if 0 <= i + by * GROUP < total]
        return lax.ppermute(value, ALL, pairs)

    def all_weights(stacks, spot):
        if not pairwise:
            return [[lax.all_gather(w[layer], "x", axis=0, tiled=True) for w in stacks] for layer in range(LAYERS)]
        place = lax.axis_index(DP)
        result = []
        for layer in range(LAYERS):
            base = stacks[0].shape[1]

            def halved(w):
                tall = w.shape[1] // 2
                piece = lax.dynamic_slice(w, (layer, spot["c"] * tall, 0), (1, tall, w.shape[2]))[0]
                came = flip(piece, "x", 1)
                return came, flip(came, "c", 1)

            share = base // (total // 2)
            parts = [lax.dynamic_slice(w, (layer, place * share, 0), (1, share, w.shape[2]))[0] for w in stacks[1:3]]
            rest = jnp.concatenate(parts, axis=1)
            rest = flip(rest, "x", 1)
            rest = lax.all_gather(rest, DP, axis=0, tiled=True)
            result.append((halved(stacks[0]), rest, halved(stacks[3])))
        return result

    def swap_core(value):
        return flip(value, "c", 1)

    def rows_for_partner(rows, spot):
        quarter = rows.shape[1] // 4
        parts = [lax.dynamic_slice_in_dim(rows, (2 * n + 1 - spot["c"]) * quarter, quarter, 1) for n in range(2)]
        return jnp.concatenate(parts, axis=1)

    def grad_first(mine, theirs, cols, units, spot):
        cols2 = swap_core(cols)
        result = {}
        for unit in units:
            _, first, steps = UNITS[unit]
            away = block_grad(mine, theirs, cols, cols2, jnp.stack([1 - spot["x"], spot["c"]]), first, steps)
            came = flip(away, "x", 1)
            result[unit] = (mine, theirs, cols, cols2, came)
        return result

    def grad_group(firsts, group, layer, spot):
        units = GROUPS[group]
        whole = sum(firsts[unit][4].shape[1] for unit in units)
        here = jnp.stack([spot["x"], spot["c"], spot["y"]])
        pair = None
        at = 0
        for unit in units:
            _, first, steps = UNITS[unit]
            pair = block_grad(*firsts[unit][:4], here, first, steps, firsts[unit][4], pair, at, whole)
            at += firsts[unit][4].shape[1]
        held, away = pair
        came = flip(away, "y", 1)
        pieces = list(sum_y(held, came, jnp.stack([spot["z"] ^ n for n in range(4)])))
        for n in (1, 2, 3):
            pieces[n] = flip(pieces[n], "z", n)
        share = sum_z(pieces)
        if (group, layer) not in BY_HAND:
            gathered = lax.all_gather(share, DP, axis=0, tiled=False)
            spots = list(range(4)) + [b % 2 for b in range(4)] + [b // 2 for b in range(4)]
            return [(gathered.reshape((4, 4) + share.shape), True, jnp.array(spots, jnp.int32))]
        near = [share]
        for n in (1, 2, 3):
            near.append(flip(share, "z", n))
        near = jnp.stack(near)
        mine = jnp.stack([near, flip(near, "y", 1)])
        theirs = flip(mine, "c", 1)
        zs = [spot["z"] ^ n for n in range(4)]
        ys = [spot["y"], 1 - spot["y"]]
        return [(mine, False, jnp.stack(zs + [spot["c"]] * 2 + ys)), (theirs, False, jnp.stack(zs + [1 - spot["c"]] * 2 + ys))]

    def plain_grad(rows, cols, whole):
        part = lax.psum_scatter(tn(rows, cols).astype(BF), "x", scatter_dimension=0, tiled=True)
        part = lax.psum(part, DP).astype(F32)[None]
        return part if whole is None else jnp.concatenate([part, whole], axis=0)

    def total_vector(vector):
        if not pairwise:
            return lax.psum(vector, ALL)
        for axis, bit in (("c", 1), ("y", 1), ("x", 1), ("z", 1), ("z", 2)):
            came = flip(vector, axis, bit)
            vector = vector + came
        return vector

    def gather_group(value):
        for name in reversed(group_axes):
            step = 1
            while step < sizes[name]:
                came = flip(value, name, step)
                first = (lax.axis_index(name) // step) % 2 == 0
                value = jnp.concatenate([jnp.where(first, value, came), jnp.where(first, came, value)])
                step *= 2
        return value

    def swap_group(blocks):
        return lax.all_to_all(blocks, group_axes, split_axis=0, concat_axis=0, tiled=True)

    def to_heads(stacked):
        count, kinds, width = stacked.shape
        blocks = stacked.reshape(count, kinds, GROUP, width // GROUP).transpose(2, 0, 1, 3)
        return swap_group(blocks.reshape(GROUP * count, kinds * (width // GROUP)))

    def to_tokens(heads, kinds):
        swapped = lax.all_to_all(heads, group_axes, split_axis=0, concat_axis=0, tiled=True)
        count = heads.shape[0] // GROUP
        blocks = swapped.reshape(GROUP, count, kinds, heads.shape[1] // kinds)
        return blocks.transpose(1, 2, 0, 3).reshape(count, kinds * GROUP * (heads.shape[1] // kinds))

    def local(
        tokens,
        image_ids,
        pad_mask,
        cotangent,
        w_qkv,
        w_out,
        w_fc1,
        w_fc2,
        b_fc1,
        proj_bias,
        value_bias,
        ln_gain,
        ln_shift,
        layer_scale,
    ):
        count, width = tokens.shape
        halo = REACH * count
        spot = {name: lax.axis_index(name) for name in ALL}
        x = spot["x"]
        place = lax.axis_index(ALL)

        own_ids = jnp.where(
            pad_mask == 1, image_ids, (1 << 20) + place * count + jnp.arange(count, dtype=jnp.int32)
        )
        qid = gather_group(own_ids)
        group = place // GROUP
        before_ids = shift_groups(qid[-halo:], 1)
        after_ids = shift_groups(qid[:halo], -1)
        before_ids = jnp.where(group == 0, -1, before_ids)
        after_ids = jnp.where(group == total // GROUP - 1, -1, after_ids)
        kid = jnp.concatenate([before_ids, qid, after_ids])
        span = kid.shape[0]
        qblk = qid.reshape(GROUP, count)
        where = jnp.arange(span, dtype=jnp.int32)[None]
        first = jnp.min(jnp.where(kid[None] == qblk[:, :1], where, span), axis=1)
        last = jnp.max(jnp.where(kid[None] == qblk[:, -1:], where, 0), axis=1)
        lo = first // LANES
        hi = last // LANES + 1
        qid_col = qid[:, None]
        qid_row = jnp.concatenate([qblk, qblk], axis=1)[:, None, :]
        kid_col = kid[:, None]
        kid_row = kid.reshape(span // LANES, 1, LANES)

        vectors = (b_fc1, proj_bias, value_bias, ln_gain, ln_shift, layer_scale)
        packed = jnp.concatenate([v.reshape(-1) for v in vectors])
        if pairwise:
            came = flip(packed, "x", 1)
            packed = jnp.stack([jnp.where(x == 0, packed, came), jnp.where(x == 0, came, packed)])
        else:
            packed = lax.all_gather(packed, "x", axis=0, tiled=False)
        shards = packed.shape[0]
        full = []
        at = 0
        for v in vectors:
            part = packed[:, at : at + v.size].reshape((shards,) + v.shape)
            at += v.size
            part = jnp.moveaxis(part, 0, -2)
            full.append(part.reshape(v.shape[:-1] + (shards * v.shape[-1],)).astype(F32))
        fc1_bias, bias, value_shift, gain, shift, scale = full

        weights = all_weights((w_qkv, w_out, w_fc1, w_fc2), spot)
        hidden_size = fc1_bias.shape[1]
        mat_at = (0, 0, width)
        whole_row = lambda size: pl.BlockSpec((count, size), lambda j, x: (0, 0))
        col_block = lambda size: pl.BlockSpec((count, size), lambda j, x: (0, j))
        kind = jax.ShapeDtypeStruct
        half = width // 2
        near, far = x * half, (1 - x) * half
        two_starts = jnp.stack([near, far])
        qkv_starts = jnp.stack([near] + [far + n * (half // 2) for n in (spot["c"], 1 - spot["c"])])
        fc2_subs = hidden_size // width
        fc2_starts = fc2_subs * qkv_starts

        residual = tokens.astype(F32)
        kept = []
        for layer in range(LAYERS):
            normed_in = layer_norm(residual, gain[layer, 0], shift[layer, 0]).astype(BF)
            added = jnp.concatenate([bias[layer, 0], jnp.zeros_like(bias[layer, 0]), value_shift[layer]])
            if pairwise:
                first_w, rest_w, last_w = weights[layer]
                heads = product(
                    qkv_kernel, normed_in, w_qkv, layer, [(w, half // 2, 0) for w in first_w], qkv_starts, width, added,
                    pl.BlockSpec((GROUP, count, 2 * HD), lambda j, x: (0, 0, j)), kind((GROUP, count, 6 * HD), BF),
                )
                heads = swap_group(heads.reshape(GROUP * count, 6 * HD))
            else:
                projected = nn(normed_in, weights[layer][0])
                heads = to_heads((projected + added).astype(BF).reshape(count, 3, width))
            kv_own = heads[:, 2 * HD :]
            before = shift_groups(kv_own[-halo:], 1)
            after = shift_groups(kv_own[:halo], -1)
            kv_win = jnp.concatenate([before, kv_own, after], axis=0)
            mixed_heads, mixed_f, lse = attn_fwd(heads, kv_win, qid_col, kid_row, lo, hi)
            mixed = to_tokens(mixed_heads, 1)
            if pairwise:
                branch_attn = product(
                    plain_kernel, mixed, w_out, layer, [(rest_w, half, mat_at[1])], two_starts, width // 2, bias[layer, 1],
                    col_block(width // 2), kind((count, width), F32),
                )
            else:
                branch_attn = nn(mixed, weights[layer][1]) + bias[layer, 1]
            middle = residual + scale[layer, 0] * branch_attn
            normed_mid = layer_norm(middle, gain[layer, 1], shift[layer, 1]).astype(BF)
            if pairwise:
                active, slope = product(
                    fc1_kernel, normed_mid, w_fc1, layer, [(rest_w, half, mat_at[2])], two_starts, width // 2, fc1_bias[layer],
                    [col_block(width // 2)] * 2, [kind((count, hidden_size), BF)] * 2,
                )
                branch_mlp = product(
                    plain_kernel, active, w_fc2, layer, [(w, hidden_size // 4, 0) for w in last_w],
                    fc2_starts, width // 2, bias[layer, 2], col_block(width // 2), kind((count, width), F32),
                )
            else:
                active, slope = gelu_parts(nn(normed_mid, weights[layer][2]) + fc1_bias[layer])
                active, slope = active.astype(BF), slope.astype(BF)
                branch_mlp = nn(active, weights[layer][3]) + bias[layer, 2]
            partner = (None,) * 4
            if pairwise:
                partner = tuple(
                    swap_core(rows_for_partner(t, spot)) for t in (normed_in, mixed, normed_mid, active)
                )
            kept.append(
                (residual, normed_in, heads, kv_win, mixed_f, lse, mixed, branch_attn, middle, normed_mid, slope, active, branch_mlp, partner)
            )
            residual = middle + scale[layer, 1] * branch_mlp
        output = residual.astype(BF)

        grad_res = cotangent.astype(F32)
        big = [None] * 4
        small = [None] * LAYERS
        for layer in reversed(range(LAYERS)):
            (
                residual, normed_in, heads, kv_win, mixed_f, lse, mixed, branch_attn, middle, normed_mid, slope, active, branch_mlp, partner
            ) = kept[layer]
            g_scale_mlp = jnp.sum(grad_res * branch_mlp, axis=0)
            g_mlp = (scale[layer, 1] * grad_res).astype(BF)
            g_bias_mlp = jnp.sum(g_mlp.astype(F32), axis=0)
            if pairwise:
                first_w, rest_w, last_w = weights[layer]
                sub = hidden_size // 2 // (hidden_size // width)
                g_hidden, g_fc1_bias = pl.pallas_call(
                    gact_kernel,
                    grid_spec=pltpu.PrefetchScalarGridSpec(
                        num_scalar_prefetch=1,
                        grid=(hidden_size // width,),
                        in_specs=[
                            whole_row(width),
                            pl.BlockSpec((1, sub, width), lambda k, x: (layer, k, 0)),
                            *[pl.BlockSpec((sub // 2, width), lambda k, x: (k, 0))] * 2,
                            whole_row(hidden_size),
                        ],
                        out_specs=[whole_row(hidden_size), pl.BlockSpec((1, hidden_size), lambda k, x: (0, 0))],
                    ),
                    out_shape=[kind((count, hidden_size), BF), kind((1, hidden_size), F32)],
                    cost_estimate=pl.CostEstimate(
                        flops=2 * count * width * hidden_size, bytes_accessed=2 * width * hidden_size, transcendentals=0
                    ),
                )(fc2_starts, g_mlp, w_fc2, *last_w, slope)
                g_fc1_bias = g_fc1_bias[0]
                firsts = grad_first(active, partner[FC2], g_mlp, (FC2A, FC2B), spot)
                g_normed_mid = product_back(
                    dx_plain_kernel, g_hidden, col_block(width), w_fc1, layer, [(rest_w, half, mat_at[2])], two_starts, width,
                    whole_row(width), kind((count, width), F32),
                )
                firsts |= grad_first(normed_mid, partner[FC1], g_hidden, (FC1A, FC1B), spot)
            else:
                g_hidden = (nt(g_mlp, weights[layer][3]) * slope.astype(F32)).astype(BF)
                g_fc1_bias = jnp.sum(g_hidden.astype(F32), axis=0)
                g_normed_mid = nt(g_hidden, weights[layer][2])
                big[3] = plain_grad(active, g_mlp, big[3])
                big[2] = plain_grad(normed_mid, g_hidden, big[2])
            _, norm_pull = jax.vjp(layer_norm, middle, gain[layer, 1], shift[layer, 1])
            g_middle, g_gain_mid, g_shift_mid = norm_pull(g_normed_mid)
            g_middle = grad_res + g_middle
            g_scale_attn = jnp.sum(g_middle * branch_attn, axis=0)
            g_attn = (scale[layer, 0] * g_middle).astype(BF)
            g_bias_attn = jnp.sum(g_attn.astype(F32), axis=0)
            if pairwise:
                g_mixed = product_back(
                    dx_out_kernel, g_attn, col_block(width // 2), w_out, layer, [(rest_w, half, mat_at[1])], two_starts, width // 2,
                    pl.BlockSpec((GROUP, count, 2 * HD), lambda j, x: (0, 0, 0)), kind((GROUP, count, 2 * HD), BF),
                    [pltpu.VMEM((count, width), F32)],
                )
                g_heads = swap_group(g_mixed.reshape(GROUP * count, 2 * HD))
                firsts |= grad_first(mixed, partner[OUT], g_attn, (NOUT,), spot)
            else:
                g_heads = to_heads(nt(g_attn, weights[layer][1]).astype(BF)[:, None, :])
                big[1] = plain_grad(mixed, g_attn, big[1])
            g_q, g_kv, g_before, g_after = attn_bwd(heads, kv_win, g_heads, qid_row, kid_col, lse, mixed_f, lo, hi)
            from_after = shift_groups(g_before, -1).astype(F32)
            from_before = shift_groups(g_after, 1).astype(F32)
            rest = GROUP * count - halo
            g_kv = g_kv + jnp.pad(from_after, ((rest, 0), (0, 0))) + jnp.pad(from_before, ((0, rest), (0, 0)))
            g_qkv_heads = jnp.concatenate([g_q, g_kv.astype(BF)], axis=1)
            if pairwise:
                g_swapped = swap_group(g_qkv_heads).reshape(GROUP, count, 6 * HD)
                g_normed_in, g_proj = product_back(
                    dx_qkv_kernel, g_swapped, pl.BlockSpec((GROUP, count, 2 * HD), lambda j, x: (0, 0, j)),
                    w_qkv, layer, [(w, half // 2, 0) for w in first_w], qkv_starts, width,
                    [whole_row(width), col_block(width)], [kind((count, width), F32), kind((count, 3 * width), BF)],
                )
                firsts |= grad_first(normed_in, partner[QKV], g_proj, (NQKV,) if GQ in USED[layer] else (NQ, NKV), spot)
                out_span, qkv_wide = (0, 1, width, None), 3 * width
                spans = {
                    G2: ((FC2, (0, fc2_subs, width, None)),),
                    G1: ((FC1, (0, 1, hidden_size, None)),),
                    GQ: ((OUT, out_span), (QKV, (width, 1, qkv_wide, None))),
                    GA: ((OUT, out_span), (QKV, (width, 1, qkv_wide, 0))),
                    GB: ((QKV, (0, 1, qkv_wide, 1)),),
                }
                for group in USED[layer]:
                    mats, cut = zip(*spans[group], strict=True)
                    for gathered, z_major, spots in grad_group(firsts, group, layer, spot):
                        placed = place_rows(gathered, z_major, spots, cut, layer, [big[m] for m in mats])
                        for m, value in zip(mats, placed, strict=True):
                            big[m] = value
            else:
                g_proj = to_tokens(g_qkv_heads, 3)
                g_normed_in = nt(g_proj, weights[layer][0])
                big[0] = plain_grad(normed_in, g_proj, big[0])
            g_bias_query = jnp.sum(g_proj[:, :width].astype(F32), axis=0)
            g_value = jnp.sum(g_proj[:, 2 * width :].astype(F32), axis=0)
            _, first_pull = jax.vjp(layer_norm, residual, gain[layer, 0], shift[layer, 0])
            g_input, g_gain_in, g_shift_in = first_pull(g_normed_in)
            grad_res = g_middle + g_input
            small[layer] = (
                jnp.concatenate(
                    [
                        g_fc1_bias,
                        g_bias_query,
                        g_bias_attn,
                        g_bias_mlp,
                        g_value,
                        g_gain_in,
                        g_gain_mid,
                        g_shift_in,
                        g_shift_mid,
                        g_scale_attn,
                        g_scale_mlp,
                    ]
                )
            )

        stacked = [b.reshape(w.shape) for b, w in zip(big, (w_qkv, w_out, w_fc1, w_fc2), strict=True)]
        sums = total_vector(jnp.stack(small))
        at = 0
        for v in vectors:
            lead = v.shape[1:-1]
            wide = shards * v.shape[-1]
            size = wide
            for n in lead:
                size *= n
            part = sums[:, at : at + size].reshape((LAYERS,) + lead + (wide,))
            at += size
            stacked.append(lax.dynamic_slice_in_dim(part, x * v.shape[-1], v.shape[-1], part.ndim - 1))
        return (output, grad_res.astype(BF), *stacked)

    return local


def solution(mesh):
    dp, fsdp = mesh.shape["dp"], mesh.shape["fsdp"]
    sizes = {"z": dp // 4, "y": 2, "c": 2, "x": fsdp}
    fine = Mesh(mesh.devices.reshape(tuple(sizes.values())), ALL)
    token = P(ALL)
    rows = P(ALL, None)
    vec2, vec3, mat = P(None, "x"), P(None, None, "x"), P(None, "x", None)
    in_specs = (rows, token, token, rows, mat, mat, mat, mat, vec2, vec3, vec2, vec3, vec3, vec3)
    out_specs = (rows, rows, mat, mat, mat, mat, vec2, vec3, vec2, vec3, vec3, vec3)
    return jax.shard_map(build(sizes), mesh=fine, in_specs=in_specs, out_specs=out_specs, check_vma=False)
```

```python
import jax
import jax.numpy as jnp
from jax import lax
from jax.experimental import pallas as pl
from jax.experimental.pallas import tpu as pltpu
from jax.sharding import Mesh
from jax.sharding import PartitionSpec as P


HD = 64
LAYERS = 2
REACH = 6
GROUP = 8
LANES = 128
KEYS = 1536
KEYS_BACK = 1536
BF = jnp.bfloat16
F32 = jnp.float32
ALL = ("z", "y", "c", "x")

QKV, OUT, FC1, FC2 = range(4)
UNITS = ((QKV, 0, 3), (QKV, 0, 1), (QKV, 1, 2), (OUT, 0, 1), (FC1, 0, 2), (FC1, 2, 2), (FC2, 0, 2), (FC2, 2, 2))
NQKV, NQ, NKV, NOUT, FC1A, FC1B, FC2A, FC2B = range(8)
GROUPS = ((FC1A, FC1B, NOUT, NQKV), (FC1A, FC1B), (FC2A, FC2B), (NOUT, NQ), (NKV,))
GM, G1, G2, GA, GB = range(5)
USED = ((G2, G1, GA, GB), (G2, GM))
BY_HAND = ((G2, 0), (GA, 0), (GB, 0))


DP = ("z", "y", "c")


def layer_norm(values, gain_row, shift_row):
    centre = values - jnp.mean(values, axis=-1, keepdims=True)
    spread = jnp.mean(centre * centre, axis=-1, keepdims=True)
    return centre * lax.rsqrt(spread + 1e-06) * gain_row + shift_row


def nn(a, b):
    return lax.dot_general(a, b, (((1,), (0,)), ((), ())), preferred_element_type=F32)


def nt(a, b):
    return lax.dot_general(a, b, (((1,), (1,)), ((), ())), preferred_element_type=F32)


def tn(a, b):
    return lax.dot_general(a, b, (((0,), (0,)), ((), ())), preferred_element_type=F32)


def masked_heads(value, low):
    return jnp.concatenate([jnp.where(low, value, 0.0), jnp.where(low, 0.0, value)], axis=0).astype(BF)


def key_range(lo_ref, hi_ref, blocks, chunk):
    i = pl.program_id(0)
    trips = (hi_ref[i] - lo_ref[i] + chunk - 1) // chunk
    return jnp.minimum(lo_ref[i], blocks - trips * chunk), trips


def attn_fwd_kernel(lo_ref, hi_ref, q_ref, k_ref, v_ref, qid_ref, kid_ref, o_ref, of_ref, lse_ref, s_scr, m_scr, l_scr, a_scr):
    blk = q_ref.shape[0]
    span = s_scr.shape[2]
    chunk = span // LANES
    low = lax.broadcasted_iota(jnp.int32, (blk, 2 * HD), 1) < HD
    q2 = masked_heads(q_ref[...].astype(F32) * 0.125, low)
    qid = qid_ref[...]
    qid2 = jnp.broadcast_to(jnp.concatenate([qid, qid], axis=0), (2 * blk, LANES))
    lo, trips = key_range(lo_ref, hi_ref, kid_ref.shape[0], chunk)
    m_scr[...] = jnp.full_like(m_scr, -1e30)
    l_scr[...] = jnp.zeros_like(l_scr)
    a_scr[...] = jnp.zeros_like(a_scr)

    def scores(t, carry):
        at = lo + t * chunk
        s = nt(q2, k_ref[pl.ds(pl.multiple_of(at * LANES, LANES), span), :])
        top = m_scr[...]
        for part in range(chunk):
            cols = slice(part * LANES, (part + 1) * LANES)
            piece = jnp.where(qid2 == kid_ref[at + part], s[:, cols], -1e30)
            s_scr[t, :, cols] = piece
            top = jnp.maximum(top, piece)
        m_scr[...] = top
        return carry

    lax.fori_loop(0, trips, scores, 0)
    row_top = jnp.max(m_scr[...], axis=1, keepdims=True)
    top = jnp.broadcast_to(row_top, (2 * blk, LANES))

    def mix(t, carry):
        v = v_ref[pl.ds(pl.multiple_of((lo + t * chunk) * LANES, LANES), span), :]
        total = l_scr[...]
        probs = []
        for part in range(chunk):
            p = jnp.exp(s_scr[t, :, part * LANES : (part + 1) * LANES] - top)
            total = total + p
            probs.append(p.astype(BF))
        l_scr[...] = total
        a_scr[...] += nn(jnp.concatenate(probs, axis=1), v)
        return carry

    lax.fori_loop(0, trips, mix, 0)
    row_total = jnp.sum(l_scr[...], axis=1, keepdims=True)
    out = a_scr[...] / row_total
    mixed = jnp.where(low, out[:blk], out[blk:])
    o_ref[...] = mixed.astype(BF)
    of_ref[...] = mixed
    lse = jnp.broadcast_to(row_top + jnp.log(row_total), (2 * blk, LANES))
    lse_ref[0] = jnp.transpose(lse)[0:1, :]


def attn_fwd(qkv, kv_win, qid_col, kid_row, lo, hi):
    rows = qkv.shape[0]
    blk = rows // lo.shape[0]
    span = kv_win.shape[0]
    wide = 2 * HD
    most = -(-((2 * REACH + 1) * blk + LANES) // KEYS)
    pairs = rows * blk * 7 * 2
    return pl.pallas_call(
        attn_fwd_kernel,
        grid_spec=pltpu.PrefetchScalarGridSpec(
            num_scalar_prefetch=2,
            grid=(rows // blk,),
            in_specs=[
                pl.BlockSpec((blk, wide), lambda i, lo, hi: (i, 0)),
                pl.BlockSpec((span, wide), lambda i, lo, hi: (0, 0)),
                pl.BlockSpec((span, wide), lambda i, lo, hi: (0, 1)),
                pl.BlockSpec((blk, 1), lambda i, lo, hi: (i, 0)),
                pl.BlockSpec(kid_row.shape, lambda i, lo, hi: (0, 0, 0)),
            ],
            out_specs=[
                pl.BlockSpec((blk, wide), lambda i, lo, hi: (i, 0)),
                pl.BlockSpec((blk, wide), lambda i, lo, hi: (i, 0)),
                pl.BlockSpec((1, 1, 2 * blk), lambda i, lo, hi: (i, 0, 0)),
            ],
            scratch_shapes=[pltpu.VMEM((most, 2 * blk, KEYS), F32)] + [pltpu.VMEM((2 * blk, LANES), F32)] * 3,
        ),
        out_shape=[
            jax.ShapeDtypeStruct((rows, wide), BF),
            jax.ShapeDtypeStruct((rows, wide), F32),
            jax.ShapeDtypeStruct((rows // blk, 1, 2 * blk), F32),
        ],
        cost_estimate=pl.CostEstimate(
            flops=pairs * wide * 4, bytes_accessed=span * wide * 4 + rows * wide * 8, transcendentals=pairs
        ),
        name="attn_fwd",
    )(lo, hi, qkv, kv_win, kv_win, qid_col, kid_row)


def attn_bwd_kernel(
    lo_ref, hi_ref, q_ref, k_ref, v_ref, do_ref, qid_ref, kid_ref, lse_ref, of_ref, dq_ref, own_ref, prev_ref, next_ref, dk_scr, dv_scr, dq_scr
):
    blk = q_ref.shape[0]
    i = pl.program_id(0)
    halo = prev_ref.shape[0]
    rows = own_ref.shape[0]
    wide = 2 * HD
    low = lax.broadcasted_iota(jnp.int32, (blk, wide), 1) < HD

    @pl.when(i == 0)
    def _():
        dk_scr[...] = jnp.zeros_like(dk_scr)
        dv_scr[...] = jnp.zeros_like(dv_scr)

    q2 = masked_heads(q_ref[...].astype(F32) * 0.125, low)
    grad = do_ref[...].astype(F32)
    g2 = masked_heads(grad, low)
    picks = jnp.where(lax.broadcasted_iota(jnp.int32, (8, wide), 1) < HD, 1.0, 0.0)
    dots = [
        lax.dot_general(
            pick, grad * of_ref[...], (((1,), (1,)), ((), ())), precision=lax.Precision.HIGHEST, preferred_element_type=F32
        )
        for pick in (picks, 1.0 - picks)
    ]
    dd = jnp.concatenate([d[0:1] for d in dots], axis=1)
    qid = qid_ref[0]
    lse = lse_ref[0]
    chunk = KEYS_BACK // LANES
    lo, trips = key_range(lo_ref, hi_ref, k_ref.shape[0] // LANES, chunk)
    dq_scr[...] = jnp.zeros_like(dq_scr)

    def step(t, carry):
        at = pl.ds(pl.multiple_of((lo + t * chunk) * LANES, LANES), KEYS_BACK)
        k = k_ref[at, :]
        v = v_ref[at, :]
        s = nt(k, q2)
        p = jnp.where(kid_ref[at, :] == qid, jnp.exp(s - lse), 0.0)
        dp = nt(v, g2)
        ds = (p * (dp - dd)).astype(BF)
        dv_scr[at, :] += nn(p.astype(BF), g2)
        dk_scr[at, :] += nn(ds, q2)
        dq_scr[...] += tn(ds, k)
        return carry

    lax.fori_loop(0, trips, step, 0)
    dq = dq_scr[...]
    dq_ref[...] = (jnp.where(low, dq[:blk], dq[blk:]) * 0.125).astype(BF)

    @pl.when(i == pl.num_programs(0) - 1)
    def _():
        for side, scr in enumerate((dk_scr, dv_scr)):
            cols = pl.ds(side * wide, wide)
            prev_ref[:, cols] = scr[pl.ds(0, halo), :].astype(BF)
            own_ref[:, cols] = scr[pl.ds(halo, rows), :]
            next_ref[:, cols] = scr[pl.ds(halo + rows, halo), :].astype(BF)


def attn_bwd(qkv, kv_win, grad_out, qid_row, kid_col, lse, mixed, lo, hi):
    rows = qkv.shape[0]
    blk = rows // qid_row.shape[0]
    span = kv_win.shape[0]
    halo = (span - rows) // 2
    wide = 2 * HD
    pairs = rows * blk * 7 * 2
    row_spec = pl.BlockSpec((1, 1, 2 * blk), lambda i, lo, hi: (i, 0, 0))
    return pl.pallas_call(
        attn_bwd_kernel,
        grid_spec=pltpu.PrefetchScalarGridSpec(
            num_scalar_prefetch=2,
            grid=(rows // blk,),
            in_specs=[
                pl.BlockSpec((blk, wide), lambda i, lo, hi: (i, 0)),
                pl.BlockSpec((span, wide), lambda i, lo, hi: (0, 0)),
                pl.BlockSpec((span, wide), lambda i, lo, hi: (0, 1)),
                pl.BlockSpec((blk, wide), lambda i, lo, hi: (i, 0)),
                row_spec,
                pl.BlockSpec((span, 1), lambda i, lo, hi: (0, 0)),
                row_spec,
                pl.BlockSpec((blk, wide), lambda i, lo, hi: (i, 0)),
            ],
            out_specs=[
                pl.BlockSpec((blk, wide), lambda i, lo, hi: (i, 0)),
                pl.BlockSpec((rows, 2 * wide), lambda i, lo, hi: (0, 0)),
                pl.BlockSpec((halo, 2 * wide), lambda i, lo, hi: (0, 0)),
                pl.BlockSpec((halo, 2 * wide), lambda i, lo, hi: (0, 0)),
            ],
            scratch_shapes=[pltpu.VMEM((span, wide), F32)] * 2 + [pltpu.VMEM((2 * blk, wide), F32)],
        ),
        out_shape=[
            jax.ShapeDtypeStruct((rows, wide), BF),
            jax.ShapeDtypeStruct((rows, 2 * wide), F32),
            jax.ShapeDtypeStruct((halo, 2 * wide), BF),
            jax.ShapeDtypeStruct((halo, 2 * wide), BF),
        ],
        cost_estimate=pl.CostEstimate(
            flops=pairs * wide * 10, bytes_accessed=span * wide * 12 + rows * wide * 12, transcendentals=pairs
        ),
        name="attn_bwd",
    )(lo, hi, qkv, kv_win, kv_win, grad_out, qid_row, kid_col, lse, mixed)


def lanes(start, size):
    return pl.ds(pl.multiple_of(start, 128), size)


def gelu_parts(values):
    share = 0.5 * (1.0 + lax.erf(values * 0.7071067811865476))
    slope = share + values * (0.3989422804014327 * jnp.exp(-0.5 * values * values))
    return values * share, slope


def halves_sum(start_ref, acts_ref, own_ref, other_refs):
    total = nn(acts_ref[:, lanes(start_ref[0], own_ref.shape[1])], own_ref[0])
    for k, ref in enumerate(other_refs):
        total += nn(acts_ref[:, lanes(start_ref[k + 1], ref.shape[0])], ref[...])
    return total


def qkv_kernel(start_ref, acts_ref, own_ref, *refs):
    others, bias_ref, out_ref = refs[:-2], refs[-2], refs[-1]
    proj = halves_sum(start_ref, acts_ref, own_ref, others) + bias_ref[0]
    wide = out_ref.shape[2]
    for g in range(GROUP):
        out_ref[g] = proj[:, g * wide : (g + 1) * wide].astype(BF)


def fc1_kernel(start_ref, acts_ref, own_ref, *refs):
    others, bias_ref, active_ref, slope_ref = refs[:-3], *refs[-3:]
    value, slope = gelu_parts(halves_sum(start_ref, acts_ref, own_ref, others) + bias_ref[0])
    active_ref[...] = value.astype(BF)
    slope_ref[...] = slope.astype(BF)


def plain_kernel(start_ref, acts_ref, own_ref, *refs):
    others, bias_ref, out_ref = refs[:-2], refs[-2], refs[-1]
    out_ref[...] = halves_sum(start_ref, acts_ref, own_ref, others) + bias_ref[0]


def other_spec(tall, wide, at):
    first = at // wide
    return pl.BlockSpec((tall, wide), lambda j, start: (0, first + j))


def product(kernel, acts, own, layer, others, starts, wide, bias, out_specs, out_shape):
    tokens = acts.shape[0]
    tall, width = own.shape[1:]
    steps = width // wide
    return pl.pallas_call(
        kernel,
        grid_spec=pltpu.PrefetchScalarGridSpec(
            num_scalar_prefetch=1,
            grid=(steps,),
            in_specs=[
                pl.BlockSpec(acts.shape, lambda j, start: (0, 0)),
                pl.BlockSpec((1, tall, wide), lambda j, start: (layer, 0, j)),
                *[other_spec(rows, wide, at) for _, rows, at in others],
                pl.BlockSpec((1, 1, wide), lambda j, start: (j, 0, 0)),
            ],
            out_specs=out_specs,
        ),
        out_shape=out_shape,
        cost_estimate=pl.CostEstimate(
            flops=4 * tokens * tall * width, bytes_accessed=4 * tall * width + 6 * tokens * width, transcendentals=0
        ),
    )(starts, acts, own, *[array for array, _, _ in others], bias.reshape(steps, 1, wide))


def gact_kernel(start_ref, grad_ref, own_ref, *refs):
    others, slope_ref, out_ref, sum_ref = refs[:-3], *refs[-3:]
    weights = [own_ref[0]] + [ref[...] for ref in others]
    for n, weight in enumerate(weights):
        at = lanes(start_ref[n] + pl.program_id(0) * weight.shape[0], weight.shape[0])
        grad = (nt(grad_ref[...], weight) * slope_ref[:, at].astype(F32)).astype(BF)
        out_ref[:, at] = grad
        sum_ref[:, at] = jnp.sum(grad.astype(F32), axis=0, keepdims=True)


def dx_kernel(start_ref, grad_ref, own_ref, other_refs, out_ref):
    weights = [own_ref[0]] + [ref[...] for ref in other_refs]
    for n, weight in enumerate(weights):
        at = lanes(start_ref[n], weight.shape[0])
        term = nt(grad_ref[...], weight)

        @pl.when(pl.program_id(0) == 0)
        def _():
            out_ref[:, at] = term

        @pl.when(pl.program_id(0) > 0)
        def _():
            out_ref[:, at] += term


def dx_plain_kernel(start_ref, grad_ref, own_ref, *refs):
    dx_kernel(start_ref, grad_ref, own_ref, refs[:-1], refs[-1])


def dx_qkv_kernel(start_ref, heads_ref, own_ref, *refs):
    others, out_ref, grad_ref = refs[:-2], refs[-2], refs[-1]
    wide = heads_ref.shape[2]
    for g in range(GROUP):
        grad_ref[:, g * wide : (g + 1) * wide] = heads_ref[g]
    dx_kernel(start_ref, grad_ref, own_ref, others, out_ref)


def dx_out_kernel(start_ref, grad_ref, own_ref, *refs):
    others, out_ref, scr = refs[:-2], refs[-2], refs[-1]
    dx_kernel(start_ref, grad_ref, own_ref, others, scr)
    wide = out_ref.shape[2]

    @pl.when(pl.program_id(0) == pl.num_programs(0) - 1)
    def _():
        for g in range(GROUP):
            out_ref[g] = scr[:, g * wide : (g + 1) * wide].astype(BF)


def product_back(kernel, grad, grad_spec, own, layer, others, starts, wide, out_specs, out_shape, scratch=()):
    tall, width = own.shape[1:]
    return pl.pallas_call(
        kernel,
        grid_spec=pltpu.PrefetchScalarGridSpec(
            num_scalar_prefetch=1,
            grid=(width // wide,),
            in_specs=[
                grad_spec,
                pl.BlockSpec((1, tall, wide), lambda j, start: (layer, 0, j)),
                *[other_spec(rows, wide, at) for _, rows, at in others],
            ],
            out_specs=out_specs,
            scratch_shapes=list(scratch),
        ),
        out_shape=out_shape,
        cost_estimate=pl.CostEstimate(
            flops=1024 * tall * width, bytes_accessed=4 * tall * width + 1024 * (tall + width), transcendentals=0
        ),
    )(starts, grad, own, *[array for array, _, _ in others])


QUARTER = 256
WIDE = 1024


def split_rows(scr, side, keep_ref, away_ref):
    half = keep_ref.shape[0]
    keep_ref[...] = scr[pl.ds(pl.multiple_of(side * half, half), half), :].astype(BF)
    away_ref[...] = scr[pl.ds(pl.multiple_of((1 - side) * half, half), half), :].astype(BF)


def away_kernel(spot_ref, mine_ref, theirs_ref, cols_ref, cols2_ref, out_ref):
    out_ref[...] = (tn(mine_ref[...], cols_ref[...]) + tn(theirs_ref[...], cols2_ref[...])).astype(BF)


def keep_kernel(spot_ref, mine_ref, theirs_ref, cols_ref, cols2_ref, came_ref, *refs):
    keep_ref, away_ref, scr = refs[-3:]
    scr[...] = tn(mine_ref[...], cols_ref[...]) + tn(theirs_ref[...], cols2_ref[...]) + came_ref[...].astype(F32)
    split_rows(scr, spot_ref[2], keep_ref, away_ref)


def block_grad(mine, theirs, cols, cols2, spot, first, steps, came=None, into=None, at=0, whole=0):
    tokens, depth = mine.shape
    width = cols.shape[1]
    subs = depth // (4 * QUARTER)
    over = (lambda j: 0) if subs > 1 else (lambda j: first + j)
    sub = (lambda j: first + j) if subs > 1 else (lambda j: 0)
    col = pl.BlockSpec((tokens, WIDE), lambda j, spot: (0, over(j)))
    in_specs = [
        pl.BlockSpec((tokens, QUARTER), lambda j, spot: (0, (spot[0] * 2 + spot[1]) * subs + sub(j))),
        pl.BlockSpec((tokens, QUARTER), lambda j, spot: (0, spot[0] * subs + sub(j))),
        col,
        col,
    ]
    operands = [mine, theirs, cols, cols2]
    scratch = []
    aliases = {}
    if came is None:
        kernel = away_kernel
        out_specs = pl.BlockSpec((QUARTER, WIDE), lambda j, spot: (0, j))
        out_shape = jax.ShapeDtypeStruct((QUARTER, steps * WIDE), BF)
    else:
        kernel = keep_kernel
        in_specs.append(pl.BlockSpec((QUARTER, WIDE), lambda j, spot: (0, j)))
        operands.append(came)
        out_specs = [pl.BlockSpec((QUARTER // 2, WIDE), lambda j, spot: (0, at // WIDE + j))] * 2
        out_shape = [jax.ShapeDtypeStruct((QUARTER // 2, whole), BF)] * 2
        scratch = [pltpu.VMEM((QUARTER, WIDE), F32)]
        if into is not None:
            in_specs += [pl.BlockSpec(memory_space=pl.ANY)] * 2
            operands += into
            aliases = {6: 0, 7: 1}
    return pl.pallas_call(
        kernel,
        grid_spec=pltpu.PrefetchScalarGridSpec(
            num_scalar_prefetch=1, grid=(steps,), in_specs=in_specs, out_specs=out_specs, scratch_shapes=scratch
        ),
        out_shape=out_shape,
        input_output_aliases=aliases,
        cost_estimate=pl.CostEstimate(
            flops=4 * tokens * QUARTER * steps * WIDE, bytes_accessed=2 * tokens * (depth + 2 * width), transcendentals=0
        ),
    )(spot, *operands)


def sum_y_kernel(at_ref, held_ref, came_ref, *refs):
    outs, scr = refs[:-1], refs[-1]
    scr[...] = held_ref[...].astype(F32) + came_ref[...].astype(F32)
    tall = outs[0].shape[0]
    for n, out_ref in enumerate(outs):
        out_ref[...] = scr[pl.ds(pl.multiple_of(at_ref[n] * tall, tall), tall), :].astype(BF)


def sum_z_kernel(*refs):
    total = refs[0][...].astype(F32)
    for ref in refs[1:-1]:
        total += ref[...].astype(F32)
    refs[-1][...] = total.astype(BF)


def sum_y(held, came, order):
    tall, width = held.shape
    count = order.shape[0]
    wide = 2048
    spec = pl.BlockSpec((tall, wide), lambda j, at: (0, j))
    return pl.pallas_call(
        sum_y_kernel,
        grid_spec=pltpu.PrefetchScalarGridSpec(
            num_scalar_prefetch=1,
            grid=(width // wide,),
            in_specs=[spec, spec],
            out_specs=[pl.BlockSpec((tall // count, wide), lambda j, at: (0, j))] * count,
            scratch_shapes=[pltpu.VMEM((tall, wide), F32)],
        ),
        out_shape=[jax.ShapeDtypeStruct((tall // count, width), BF)] * count,
        cost_estimate=pl.CostEstimate(flops=tall * width, bytes_accessed=6 * tall * width, transcendentals=0),
    )(order, held, came)


def sum_z(parts):
    tall, width = parts[0].shape
    wide = 2048
    spec = pl.BlockSpec((tall, wide), lambda j: (0, j))
    return pl.pallas_call(
        sum_z_kernel,
        grid=(width // wide,),
        in_specs=[spec] * len(parts),
        out_specs=spec,
        out_shape=jax.ShapeDtypeStruct((tall, width), BF),
        cost_estimate=pl.CostEstimate(flops=4 * tall * width, bytes_accessed=10 * tall * width, transcendentals=0),
    )(*parts)


def place_kernel(spans, z_major, spot_ref, in_ref, *refs):
    outs = refs[-len(spans) :]
    count = in_ref.shape[0 if z_major else 1]
    share = in_ref.shape[2]
    for z in range(count):
        rows = pl.ds(pl.multiple_of(spot_ref[z] * share, share), share)
        for (at, subs, _, _), out_ref in zip(spans, outs, strict=True):
            wide = out_ref.shape[5]
            for k in range(subs):
                cols = slice(at + k * wide, at + (k + 1) * wide)
                piece = in_ref[z, 0, :, cols] if z_major else in_ref[0, z, :, cols]
                out_ref[0, 0, k, 0, rows, :] = piece.astype(F32)


def place_rows(gathered, z_major, spots, spans, layer, wholes):
    count, sides = gathered.shape[:2] if z_major else gathered.shape[1::-1]
    share, width = gathered.shape[2:]
    rows = count * share
    steps = width // WIDE if len(spans) == 1 and spans[0][3] is not None else 1
    part = width // steps
    block = (count, 1, share, part) if z_major else (1, count, share, part)
    shapes = [jax.ShapeDtypeStruct((LAYERS, 2, subs, 2, rows, wide), F32) for _, subs, wide, _ in spans]
    more = [] if wholes[0] is None else wholes

    def out_spec(span):
        _, subs, wide, first = span
        wide, at = (wide, 0) if first is None else (WIDE, first)
        return pl.BlockSpec(
            (1, 1, subs, 1, rows, wide), lambda b, j, spot: (layer, spot[count + b], 0, spot[count + sides + b], 0, at + j)
        )

    return pl.pallas_call(
        lambda *refs: place_kernel(spans, z_major, *refs),
        grid_spec=pltpu.PrefetchScalarGridSpec(
            num_scalar_prefetch=1,
            grid=(sides, steps),
            in_specs=[pl.BlockSpec(block, lambda b, j, spot: (0, b, 0, j) if z_major else (b, 0, 0, j))]
            + [pl.BlockSpec(memory_space=pl.ANY)] * len(more),
            out_specs=[out_spec(span) for span in spans],
        ),
        out_shape=shapes,
        input_output_aliases={n + 2: n for n in range(len(more))},
        cost_estimate=pl.CostEstimate(flops=0, bytes_accessed=6 * count * sides * share * width, transcendentals=0),
    )(spots, gathered, *more)


def build(sizes):
    group_axes = []
    reach = 1
    for name in reversed(ALL):
        if reach < GROUP:
            group_axes.insert(0, name)
            reach *= sizes[name]
    assert reach == GROUP
    group_axes = tuple(group_axes)
    total = sizes["z"] * sizes["y"] * sizes["c"] * sizes["x"]
    pairwise = sizes["x"] == 2 and sizes["z"] == 4

    def flip(value, axis, bit):
        return lax.ppermute(value, axis, [(i, i ^ bit) for i in range(sizes[axis])])

    def shift_groups(value, by):
        pairs = [(i, i + by * GROUP) for i in range(total) if 0 <= i + by * GROUP < total]
        return lax.ppermute(value, ALL, pairs)

    def all_weights(stacks, spot):
        if not pairwise:
            return [[lax.all_gather(w[layer], "x", axis=0, tiled=True) for w in stacks] for layer in range(LAYERS)]
        place = lax.axis_index(DP)
        result = []
        for layer in range(LAYERS):
            base = stacks[0].shape[1]

            def halved(w):
                tall = w.shape[1] // 2
                piece = lax.dynamic_slice(w, (layer, spot["c"] * tall, 0), (1, tall, w.shape[2]))[0]
                came = flip(piece, "x", 1)
                return came, flip(came, "c", 1)

            share = base // (total // 2)
            parts = [lax.dynamic_slice(w, (layer, place * share, 0), (1, share, w.shape[2]))[0] for w in stacks[1:3]]
            rest = jnp.concatenate(parts, axis=1)
            rest = flip(rest, "x", 1)
            rest = lax.all_gather(rest, DP, axis=0, tiled=True)
            result.append((halved(stacks[0]), rest, halved(stacks[3])))
        return result

    def swap_core(value):
        return flip(value, "c", 1)

    def rows_for_partner(rows, spot):
        quarter = rows.shape[1] // 4
        parts = [lax.dynamic_slice_in_dim(rows, (2 * n + 1 - spot["c"]) * quarter, quarter, 1) for n in range(2)]
        return jnp.concatenate(parts, axis=1)

    def grad_first(mine, theirs, cols, units, spot):
        cols2 = swap_core(cols)
        result = {}
        for unit in units:
            _, first, steps = UNITS[unit]
            away = block_grad(mine, theirs, cols, cols2, jnp.stack([1 - spot["x"], spot["c"]]), first, steps)
            came = flip(away, "x", 1)
            result[unit] = (mine, theirs, cols, cols2, came)
        return result

    def grad_group(firsts, group, layer, spot):
        units = GROUPS[group]
        whole = sum(firsts[unit][4].shape[1] for unit in units)
        here = jnp.stack([spot["x"], spot["c"], spot["y"]])
        pair = None
        at = 0
        for unit in units:
            _, first, steps = UNITS[unit]
            pair = block_grad(*firsts[unit][:4], here, first, steps, firsts[unit][4], pair, at, whole)
            at += firsts[unit][4].shape[1]
        held, away = pair
        came = flip(away, "y", 1)
        pieces = list(sum_y(held, came, jnp.stack([spot["z"] ^ n for n in range(4)])))
        for n in (1, 2, 3):
            pieces[n] = flip(pieces[n], "z", n)
        share = sum_z(pieces)
        if (group, layer) not in BY_HAND:
            gathered = lax.all_gather(share, DP, axis=0, tiled=False)
            spots = list(range(4)) + [b % 2 for b in range(4)] + [b // 2 for b in range(4)]
            return [(gathered.reshape((4, 4) + share.shape), True, jnp.array(spots, jnp.int32))]
        near = [share]
        for n in (1, 2, 3):
            near.append(flip(share, "z", n))
        near = jnp.stack(near)
        mine = jnp.stack([near, flip(near, "y", 1)])
        theirs = flip(mine, "c", 1)
        zs = [spot["z"] ^ n for n in range(4)]
        ys = [spot["y"], 1 - spot["y"]]
        return [(mine, False, jnp.stack(zs + [spot["c"]] * 2 + ys)), (theirs, False, jnp.stack(zs + [1 - spot["c"]] * 2 + ys))]

    def plain_grad(rows, cols, whole):
        part = lax.psum_scatter(tn(rows, cols).astype(BF), "x", scatter_dimension=0, tiled=True)
        part = lax.psum(part, DP).astype(F32)[None]
        return part if whole is None else jnp.concatenate([part, whole], axis=0)

    def total_vector(vector):
        if not pairwise:
            return lax.psum(vector, ALL)
        for axis, bit in (("c", 1), ("y", 1), ("x", 1), ("z", 1), ("z", 2)):
            came = flip(vector, axis, bit)
            vector = vector + came
        return vector

    def gather_group(value):
        for name in reversed(group_axes):
            step = 1
            while step < sizes[name]:
                came = flip(value, name, step)
                first = (lax.axis_index(name) // step) % 2 == 0
                value = jnp.concatenate([jnp.where(first, value, came), jnp.where(first, came, value)])
                step *= 2
        return value

    def swap_group(blocks):
        return lax.all_to_all(blocks, group_axes, split_axis=0, concat_axis=0, tiled=True)

    def to_heads(stacked):
        count, kinds, width = stacked.shape
        blocks = stacked.reshape(count, kinds, GROUP, width // GROUP).transpose(2, 0, 1, 3)
        return swap_group(blocks.reshape(GROUP * count, kinds * (width // GROUP)))

    def to_tokens(heads, kinds):
        swapped = swap_group(heads)
        count = heads.shape[0] // GROUP
        blocks = swapped.reshape(GROUP, count, kinds, heads.shape[1] // kinds)
        return blocks.transpose(1, 2, 0, 3).reshape(count, kinds * GROUP * (heads.shape[1] // kinds))

    def local(
        tokens,
        image_ids,
        pad_mask,
        cotangent,
        w_qkv,
        w_out,
        w_fc1,
        w_fc2,
        b_fc1,
        proj_bias,
        value_bias,
        ln_gain,
        ln_shift,
        layer_scale,
    ):
        count, width = tokens.shape
        halo = REACH * count
        spot = {name: lax.axis_index(name) for name in ALL}
        x = spot["x"]
        place = lax.axis_index(ALL)

        own_ids = jnp.where(
            pad_mask == 1, image_ids, (1 << 20) + place * count + jnp.arange(count, dtype=jnp.int32)
        )
        qid = gather_group(own_ids)
        group = place // GROUP
        before_ids = shift_groups(qid[-halo:], 1)
        after_ids = shift_groups(qid[:halo], -1)
        before_ids = jnp.where(group == 0, -1, before_ids)
        after_ids = jnp.where(group == total // GROUP - 1, -1, after_ids)
        kid = jnp.concatenate([before_ids, qid, after_ids])
        span = kid.shape[0]
        qblk = qid.reshape(GROUP, count)
        where = jnp.arange(span, dtype=jnp.int32)[None]
        first = jnp.min(jnp.where(kid[None] == qblk[:, :1], where, span), axis=1)
        last = jnp.max(jnp.where(kid[None] == qblk[:, -1:], where, 0), axis=1)
        lo = first // LANES
        hi = last // LANES + 1
        qid_col = qid[:, None]
        qid_row = jnp.concatenate([qblk, qblk], axis=1)[:, None, :]
        kid_col = kid[:, None]
        kid_row = kid.reshape(span // LANES, 1, LANES)

        vectors = (b_fc1, proj_bias, value_bias, ln_gain, ln_shift, layer_scale)
        packed = jnp.concatenate([v.reshape(-1) for v in vectors])
        if pairwise:
            came = flip(packed, "x", 1)
            packed = jnp.stack([jnp.where(x == 0, packed, came), jnp.where(x == 0, came, packed)])
        else:
            packed = lax.all_gather(packed, "x", axis=0, tiled=False)
        shards = packed.shape[0]
        full = []
        at = 0
        for v in vectors:
            part = packed[:, at : at + v.size].reshape((shards,) + v.shape)
            at += v.size
            part = jnp.moveaxis(part, 0, -2)
            full.append(part.reshape(v.shape[:-1] + (shards * v.shape[-1],)).astype(F32))
        fc1_bias, bias, value_shift, gain, shift, scale = full

        weights = all_weights((w_qkv, w_out, w_fc1, w_fc2), spot)
        hidden_size = fc1_bias.shape[1]
        mat_at = (0, 0, width)
        whole_row = lambda size: pl.BlockSpec((count, size), lambda j, x: (0, 0))
        col_block = lambda size: pl.BlockSpec((count, size), lambda j, x: (0, j))
        kind = jax.ShapeDtypeStruct
        half = width // 2
        near, far = x * half, (1 - x) * half
        two_starts = jnp.stack([near, far])
        qkv_starts = jnp.stack([near] + [far + n * (half // 2) for n in (spot["c"], 1 - spot["c"])])
        fc2_subs = hidden_size // width
        fc2_starts = fc2_subs * qkv_starts

        residual = tokens.astype(F32)
        kept = []
        for layer in range(LAYERS):
            normed_in = layer_norm(residual, gain[layer, 0], shift[layer, 0]).astype(BF)
            added = jnp.concatenate([bias[layer, 0], jnp.zeros_like(bias[layer, 0]), value_shift[layer]])
            if pairwise:
                first_w, rest_w, last_w = weights[layer]
                heads = product(
                    qkv_kernel, normed_in, w_qkv, layer, [(w, half // 2, 0) for w in first_w], qkv_starts, width, added,
                    pl.BlockSpec((GROUP, count, 2 * HD), lambda j, x: (0, 0, j)), kind((GROUP, count, 6 * HD), BF),
                )
                heads = swap_group(heads.reshape(GROUP * count, 6 * HD))
            else:
                projected = nn(normed_in, weights[layer][0])
                heads = to_heads((projected + added).astype(BF).reshape(count, 3, width))
            kv_own = heads[:, 2 * HD :]
            before = shift_groups(kv_own[-halo:], 1)
            after = shift_groups(kv_own[:halo], -1)
            kv_win = jnp.concatenate([before, kv_own, after], axis=0)
            mixed_heads, mixed_f, lse = attn_fwd(heads, kv_win, qid_col, kid_row, lo, hi)
            mixed = to_tokens(mixed_heads, 1)
            if pairwise:
                branch_attn = product(
                    plain_kernel, mixed, w_out, layer, [(rest_w, half, mat_at[1])], two_starts, width // 2, bias[layer, 1],
                    col_block(width // 2), kind((count, width), F32),
                )
            else:
                branch_attn = nn(mixed, weights[layer][1]) + bias[layer, 1]
            middle = residual + scale[layer, 0] * branch_attn
            normed_mid = layer_norm(middle, gain[layer, 1], shift[layer, 1]).astype(BF)
            if pairwise:
                active, slope = product(
                    fc1_kernel, normed_mid, w_fc1, layer, [(rest_w, half, mat_at[2])], two_starts, width // 2, fc1_bias[layer],
                    [col_block(width // 2)] * 2, [kind((count, hidden_size), BF)] * 2,
                )
                branch_mlp = product(
                    plain_kernel, active, w_fc2, layer, [(w, hidden_size // 4, 0) for w in last_w],
                    fc2_starts, width // 2, bias[layer, 2], col_block(width // 2), kind((count, width), F32),
                )
            else:
                active, slope = gelu_parts(nn(normed_mid, weights[layer][2]) + fc1_bias[layer])
                active, slope = active.astype(BF), slope.astype(BF)
                branch_mlp = nn(active, weights[layer][3]) + bias[layer, 2]
            partner = (None,) * 4
            if pairwise:
                partner = tuple(
                    swap_core(rows_for_partner(t, spot)) for t in (normed_in, mixed, normed_mid, active)
                )
            kept.append(
                (residual, normed_in, heads, kv_win, mixed_f, lse, mixed, branch_attn, middle, normed_mid, slope, active, branch_mlp, partner)
            )
            residual = middle + scale[layer, 1] * branch_mlp
        output = residual.astype(BF)

        grad_res = cotangent.astype(F32)
        big = [None] * 4
        small = [None] * LAYERS
        for layer in reversed(range(LAYERS)):
            (
                residual, normed_in, heads, kv_win, mixed_f, lse, mixed, branch_attn, middle, normed_mid, slope, active, branch_mlp, partner
            ) = kept[layer]
            g_scale_mlp = jnp.sum(grad_res * branch_mlp, axis=0)
            g_mlp = (scale[layer, 1] * grad_res).astype(BF)
            g_bias_mlp = jnp.sum(g_mlp.astype(F32), axis=0)
            if pairwise:
                first_w, rest_w, last_w = weights[layer]
                sub = hidden_size // 2 // (hidden_size // width)
                g_hidden, g_fc1_bias = pl.pallas_call(
                    gact_kernel,
                    grid_spec=pltpu.PrefetchScalarGridSpec(
                        num_scalar_prefetch=1,
                        grid=(hidden_size // width,),
                        in_specs=[
                            whole_row(width),
                            pl.BlockSpec((1, sub, width), lambda k, x: (layer, k, 0)),
                            *[pl.BlockSpec((sub // 2, width), lambda k, x: (k, 0))] * 2,
                            whole_row(hidden_size),
                        ],
                        out_specs=[whole_row(hidden_size), pl.BlockSpec((1, hidden_size), lambda k, x: (0, 0))],
                    ),
                    out_shape=[kind((count, hidden_size), BF), kind((1, hidden_size), F32)],
                    cost_estimate=pl.CostEstimate(
                        flops=2 * count * width * hidden_size, bytes_accessed=2 * width * hidden_size, transcendentals=0
                    ),
                )(fc2_starts, g_mlp, w_fc2, *last_w, slope)
                g_fc1_bias = g_fc1_bias[0]
                firsts = grad_first(active, partner[FC2], g_mlp, (FC2A, FC2B), spot)
                g_normed_mid = product_back(
                    dx_plain_kernel, g_hidden, col_block(width), w_fc1, layer, [(rest_w, half, mat_at[2])], two_starts, width,
                    whole_row(width), kind((count, width), F32),
                )
                firsts |= grad_first(normed_mid, partner[FC1], g_hidden, (FC1A, FC1B), spot)
            else:
                g_hidden = (nt(g_mlp, weights[layer][3]) * slope.astype(F32)).astype(BF)
                g_fc1_bias = jnp.sum(g_hidden.astype(F32), axis=0)
                g_normed_mid = nt(g_hidden, weights[layer][2])
                big[3] = plain_grad(active, g_mlp, big[3])
                big[2] = plain_grad(normed_mid, g_hidden, big[2])
            _, norm_pull = jax.vjp(layer_norm, middle, gain[layer, 1], shift[layer, 1])
            g_middle, g_gain_mid, g_shift_mid = norm_pull(g_normed_mid)
            g_middle = grad_res + g_middle
            g_scale_attn = jnp.sum(g_middle * branch_attn, axis=0)
            g_attn = (scale[layer, 0] * g_middle).astype(BF)
            g_bias_attn = jnp.sum(g_attn.astype(F32), axis=0)
            if pairwise:
                g_mixed = product_back(
                    dx_out_kernel, g_attn, col_block(width // 2), w_out, layer, [(rest_w, half, mat_at[1])], two_starts, width // 2,
                    pl.BlockSpec((GROUP, count, 2 * HD), lambda j, x: (0, 0, 0)), kind((GROUP, count, 2 * HD), BF),
                    [pltpu.VMEM((count, width), F32)],
                )
                g_heads = swap_group(g_mixed.reshape(GROUP * count, 2 * HD))
                firsts |= grad_first(mixed, partner[OUT], g_attn, (NOUT,), spot)
            else:
                g_heads = to_heads(nt(g_attn, weights[layer][1]).astype(BF)[:, None, :])
                big[1] = plain_grad(mixed, g_attn, big[1])
            g_q, g_kv, g_before, g_after = attn_bwd(heads, kv_win, g_heads, qid_row, kid_col, lse, mixed_f, lo, hi)
            from_after = shift_groups(g_before, -1).astype(F32)
            from_before = shift_groups(g_after, 1).astype(F32)
            rest = GROUP * count - halo
            g_kv = g_kv + jnp.pad(from_after, ((rest, 0), (0, 0))) + jnp.pad(from_before, ((0, rest), (0, 0)))
            g_qkv_heads = jnp.concatenate([g_q, g_kv.astype(BF)], axis=1)
            if pairwise:
                g_swapped = swap_group(g_qkv_heads).reshape(GROUP, count, 6 * HD)
                g_normed_in, g_proj = product_back(
                    dx_qkv_kernel, g_swapped, pl.BlockSpec((GROUP, count, 2 * HD), lambda j, x: (0, 0, j)),
                    w_qkv, layer, [(w, half // 2, 0) for w in first_w], qkv_starts, width,
                    [whole_row(width), col_block(width)], [kind((count, width), F32), kind((count, 3 * width), BF)],
                )
                firsts |= grad_first(normed_in, partner[QKV], g_proj, (NQKV,) if GM in USED[layer] else (NQ, NKV), spot)
                out_span, qkv_wide = (0, 1, width, None), 3 * width
                spans = {
                    G2: ((FC2, (0, fc2_subs, width, None)),),
                    G1: ((FC1, (0, 1, hidden_size, None)),),
                    GM: (
                        (FC1, (0, 1, hidden_size, None)),
                        (OUT, (hidden_size, 1, width, None)),
                        (QKV, (hidden_size + width, 1, qkv_wide, None)),
                    ),
                    GA: ((OUT, out_span), (QKV, (width, 1, qkv_wide, 0))),
                    GB: ((QKV, (0, 1, qkv_wide, 1)),),
                }
                for group in USED[layer]:
                    mats, cut = zip(*spans[group], strict=True)
                    for gathered, z_major, spots in grad_group(firsts, group, layer, spot):
                        placed = place_rows(gathered, z_major, spots, cut, layer, [big[m] for m in mats])
                        for m, value in zip(mats, placed, strict=True):
                            big[m] = value
            else:
                g_proj = to_tokens(g_qkv_heads, 3)
                g_normed_in = nt(g_proj, weights[layer][0])
                big[0] = plain_grad(normed_in, g_proj, big[0])
            g_bias_query = jnp.sum(g_proj[:, :width].astype(F32), axis=0)
            g_value = jnp.sum(g_proj[:, 2 * width :].astype(F32), axis=0)
            _, first_pull = jax.vjp(layer_norm, residual, gain[layer, 0], shift[layer, 0])
            g_input, g_gain_in, g_shift_in = first_pull(g_normed_in)
            grad_res = g_middle + g_input
            small[layer] = (
                jnp.concatenate(
                    [
                        g_fc1_bias,
                        g_bias_query,
                        g_bias_attn,
                        g_bias_mlp,
                        g_value,
                        g_gain_in,
                        g_gain_mid,
                        g_shift_in,
                        g_shift_mid,
                        g_scale_attn,
                        g_scale_mlp,
                    ]
                )
            )

        stacked = [b.reshape(w.shape) for b, w in zip(big, (w_qkv, w_out, w_fc1, w_fc2), strict=True)]
        sums = total_vector(jnp.stack(small))
        at = 0
        for v in vectors:
            lead = v.shape[1:-1]
            wide = shards * v.shape[-1]
            size = wide
            for n in lead:
                size *= n
            part = sums[:, at : at + size].reshape((LAYERS,) + lead + (wide,))
            at += size
            stacked.append(lax.dynamic_slice_in_dim(part, x * v.shape[-1], v.shape[-1], part.ndim - 1))
        return (output, grad_res.astype(BF), *stacked)

    return local


def solution(mesh):
    dp, fsdp = mesh.shape["dp"], mesh.shape["fsdp"]
    sizes = {"z": dp // 4, "y": 2, "c": 2, "x": fsdp}
    fine = Mesh(mesh.devices.reshape(tuple(sizes.values())), ALL)
    token = P(ALL)
    rows = P(ALL, None)
    vec2, vec3, mat = P(None, "x"), P(None, None, "x"), P(None, "x", None)
    in_specs = (rows, token, token, rows, mat, mat, mat, mat, vec2, vec3, vec2, vec3, vec3, vec3)
    out_specs = (rows, rows, mat, mat, mat, mat, vec2, vec3, vec2, vec3, vec3, vec3)
    return jax.shard_map(build(sizes), mesh=fine, in_specs=in_specs, out_specs=out_specs, check_vma=False)
```
